32 devices in a mesh: expert: 4 (over y, x), seq: 2 (over core), mp: 4 (over z).
Axes of the slice: x: 2, y: 2, z: 4, core: 2. Of those that a mesh axis runs over, the one named last changes fastest.
Arguments:
- queries: bfloat16 [4, 1536, 2560], P('expert', 'seq', 'mp'), may hold values from -4000 to 4000
- key_input: bfloat16 [4, 1536, 2560], P('expert', 'seq', 'mp'), may hold values from -4000 to 4000
- value_input: bfloat16 [4, 1536, 2560], P('expert', 'seq', 'mp'), may hold values from -6 to 6
- timestep: int32 [4], P('expert'), may hold values from 0 to 999
- neighbours: int32 [4, 12, 5], P('expert', 'seq'), may hold values from 0 to 11, as said below
- q_gain: float32 [2, 2560], P(None, 'mp'), may hold values from 0.1 to 1.9
- k_gain: float32 [2, 2560], P(None, 'mp'), may hold values from 0.1 to 1.9
Outputs:
- mixed: bfloat16 [4, 1536, 2560], P('expert', 'seq', 'mp')
The draws below stay inside these ranges and needn't reach their ends.
Inputs may be any that keep to these rules, and one draw needn't show every extreme that they name: For a query tile i, let d = i // 6. The 5 entries of neighbours[s, i] are distinct tile numbers from d * 6 - 1 to d * 6 + 6, and the first entry is i itself.
All inputs are finite; a program needn't handle non-finite values.
Results may differ from the reference program's by a relative error of at most 0.0099.
Values may be sent and summed in bfloat16 or wider, within the bound.
No kernel may reach another device: no remote copies, remote signals or barrier semaphores. Data moves between devices by JAX's collectives and lax.ppermute only.
A program may use at most 64 MiB of HBM per device.

```python
import math
import jax
import jax.numpy as jnp
from jax import lax

DH = 128
HEADS = 20
TILE = 128
HD = 2560
TILES_DEV = 6
NB = 5
SAMPLES = 4
L = 1536
TILES = 12


def draw_rows(key, which):
    shape = (SAMPLES, L, HEADS, DH)
    base = jnp.clip(jax.random.normal(jax.random.fold_in(key, which), shape, jnp.float32), -5.0, 5.0)
    head_scale = jnp.exp(jax.random.uniform(jax.random.fold_in(key, which + 10), (SAMPLES, 1, HEADS, 1), jnp.float32, math.log(0.3), math.log(3.0)))
    column_scale = jnp.exp(jax.random.uniform(jax.random.fold_in(key, which + 20), (1, 1, HEADS, DH), jnp.float32, math.log(0.5), math.log(2.0)))
    row_scale = jnp.exp(jax.random.uniform(jax.random.fold_in(key, which + 30), (SAMPLES, L, 1, 1), jnp.float32, math.log(0.2), math.log(5.0)))
    return base * head_scale * column_scale * row_scale


def draw_queries(key, part):
    rows = draw_rows(key, 1)
    return rows.reshape(SAMPLES, L, HEADS * DH).astype(jnp.bfloat16)


def draw_key_input(key, part):
    rows = draw_rows(key, 2)
    return rows.reshape(SAMPLES, L, HEADS * DH).astype(jnp.bfloat16)


def draw_neighbours(key, part):
    own_key = jax.random.fold_in(key, 77)
    width_window = TILES_DEV + 2
    tile_ids = jnp.arange(TILES)[:, None]
    offsets = jnp.arange(width_window)[None, :] - 1
    device_of = tile_ids // TILES_DEV
    candidates = device_of * TILES_DEV + offsets
    valid = (candidates >= 0) & (candidates < TILES)
    noise = jax.random.randint(own_key, (SAMPLES, TILES, width_window), 0, 1 << 16)
    scores = noise * 64 + jnp.arange(width_window)[None, None, :] + 64
    scores = jnp.where((candidates == tile_ids)[None, :, :], 0, scores)
    scores = jnp.where(valid[None, :, :], scores, 1 << 30)
    order = jnp.argsort(scores, axis=-1, stable=True)[:, :, :NB]
    full = jnp.broadcast_to(candidates[None, :, :], (SAMPLES, TILES, width_window))
    return jnp.take_along_axis(full, order, axis=-1).astype(jnp.int32)


def set_ends(entries, key, smallest, top_value):
    spot = [jax.random.randint(jax.random.fold_in(key, axis), (), 0, length) for axis, length in enumerate(entries.shape)]
    widest = entries.shape.index(max(entries.shape))
    beside = spot[:widest] + [(spot[widest] + 1) % entries.shape[widest]] + spot[widest + 1:]
    return entries.at[tuple(spot)].set(smallest).at[tuple(beside)].set(top_value)


def block_scale(rng, extent, shards, low, largest):
    def one(dim, parts):
        draws = jax.random.uniform(jax.random.fold_in(jax.random.fold_in(rng, 6), dim), (parts,), jnp.float32, low / len(shards), largest / len(shards))
        return jnp.repeat(jnp.exp(draws), extent[dim] // parts).reshape((-1,) + (1,) * (len(extent) - dim - 1))

    loudness = one(*shards[0])
    for cut in shards[1:]:
        loudness = loudness * one(*cut)
    return loudness


def scatter_about(stream_key, shape, width, most, pieces=(), kind=jnp.bfloat16):
    array = width * jax.random.normal(stream_key, shape, jnp.float32)
    if pieces:
        array = array * block_scale(stream_key, shape, pieces, -0.22, 0.18)
    return jnp.clip(array, -most, most).astype(kind)


def setup_inputs(seed: int = 0) -> dict:
    arg_keys = jax.random.split(jax.random.key(seed), 8)
    return {
        "queries": draw_queries(jax.random.fold_in(arg_keys[7], 71), 0),
        "key_input": draw_key_input(jax.random.fold_in(arg_keys[7], 71), 0),
        "value_input": scatter_about(arg_keys[2], (SAMPLES, L, HD), 1.0, 6.0, ((0, 4), (1, 2), (2, 4))),
        "timestep": set_ends(jax.random.randint(arg_keys[3], (SAMPLES,), 0, 1000), jax.random.fold_in(arg_keys[3], 1), 0, 999).astype(jnp.int32),
        "neighbours": draw_neighbours(jax.random.fold_in(arg_keys[7], 71), 0),
        "q_gain": jnp.clip(1.0 + 0.18 * jax.random.normal(arg_keys[5], (2, HD), jnp.float32), 0.1, 1.9),
        "k_gain": jnp.clip(1.0 + 0.18 * jax.random.normal(arg_keys[6], (2, HD), jnp.float32), 0.1, 1.9),
    }


epsilon = 1e-06
switch_step = 875

def normed(rows, gain):
    values = rows.astype(jnp.float32)
    mean_sq = lax.optimization_barrier(jnp.mean(values * values, axis=-1, keepdims=True))
    return (values * lax.rsqrt(mean_sq + epsilon) * gain).astype(jnp.bfloat16)

def reference(queries, key_input, value_input, timestep, neighbours, q_gain, k_gain):
    expert_id = jnp.where(timestep >= switch_step, 0, 1).astype(jnp.int32)
    gains_q = q_gain[expert_id]
    gains_k = k_gain[expert_id]

    def one_sample(inputs):
        q_rows, k_rows, v_rows, listed, gain_q, gain_k = inputs
        q_normed = normed(q_rows, gain_q).reshape(TILES, TILE, HEADS, DH)
        k_normed = normed(k_rows, gain_k).reshape(TILES, TILE, HEADS, DH)
        v_tiles = v_rows.reshape(TILES, TILE, HEADS, DH)

        def one_tile(index):
            query_rows = q_normed[index].astype(jnp.float32)
            chosen = listed[index]
            key_rows = k_normed[chosen].reshape(NB * TILE, HEADS, DH).astype(jnp.float32)
            values = v_tiles[chosen].reshape(NB * TILE, HEADS, DH).astype(jnp.float32)
            scores = jnp.einsum('qhd,khd->hqk', query_rows, key_rows) * DH ** (-0.5)
            top = lax.optimization_barrier(jnp.max(scores, axis=-1, keepdims=True))
            expo = jnp.exp(scores - top)
            weights = (expo / lax.optimization_barrier(jnp.sum(expo, axis=-1, keepdims=True))).astype(jnp.bfloat16)
            result = jnp.einsum('hqk,khd->qhd', weights.astype(jnp.float32), values)
            return result.astype(jnp.bfloat16).reshape(TILE, HEADS * DH)
        tiles_out = lax.map(one_tile, jnp.arange(TILES, dtype=jnp.int32))
        return tiles_out.reshape(L, HEADS * DH)
    return lax.map(one_sample, (queries, key_input, value_input, neighbours, gains_q, gains_k))
```

```python
import functools

import jax
import jax.numpy as jnp
from jax import lax
from jax.experimental import pallas as pl
from jax.experimental.pallas import tpu as pltpu
from jax.sharding import PartitionSpec as P

DH = 128
TILE = 128
EPSILON = 1e-06
SWITCH_STEP = 875
LOG2E = 1.4426950408889634
MIB = 1 << 20

HBM = pl.BlockSpec(memory_space=pltpu.HBM)
VMEM = pl.BlockSpec(memory_space=pltpu.VMEM)
SMEM = pl.BlockSpec(memory_space=pltpu.SMEM)


def tile_rows(index):
    if isinstance(index, int):
        return pl.ds(index * TILE, TILE)
    return pl.ds(pl.multiple_of(index * TILE, TILE), TILE)


def sums_kernel(chunk, edge_ref, q_hbm, k_hbm, v_hbm, sums_ref, *rest):
    edges = rest[: edge_ref.shape[0]]
    q_buf, k_buf, sems, edge_sems = rest[edge_ref.shape[0] :]
    rows, width = q_hbm.shape
    copies = []
    for a, (src, dst) in enumerate(((q_hbm, q_buf), (k_hbm, k_buf))):
        for j in range(rows // chunk):
            part = pl.ds(j * chunk, chunk)
            copies.append(pltpu.make_async_copy(src.at[part], dst.at[part], sems.at[a, j]))
            copies[-1].start()
    edge_copies = []
    for e, edge in enumerate(edges):
        part = tile_rows(edge_ref[e])
        for a, src in enumerate((k_hbm, v_hbm)):
            edge_copies.append(pltpu.make_async_copy(src.at[part], edge.at[a], edge_sems.at[e, a]))
            edge_copies[-1].start()
    diagonal = lax.broadcasted_iota(jnp.int32, (TILE, TILE), 0) == lax.broadcasted_iota(
        jnp.int32, (TILE, TILE), 1
    )
    tiles = rows // TILE
    for a, buf in enumerate((q_buf, k_buf)):
        for t in range(tiles):
            if t * TILE % chunk == 0:
                copies[a * (rows // chunk) + t * TILE // chunk].wait()
            total = 0.0
            for j in range(width // DH):
                x = buf[t * TILE : (t + 1) * TILE, j * DH : (j + 1) * DH].astype(jnp.float32)
                total = total + x * x
            total = jnp.sum(total, axis=1, keepdims=True)
            total = jnp.sum(jnp.where(diagonal, total, 0.0), axis=0, keepdims=True)
            sums_ref[a * tiles + t : a * tiles + t + 1, :] = total
    for copy in edge_copies:
        copy.wait()


def gather_kernel(q_hbm, k_hbm, v_hbm, *rest):
    edges = rest[:-4]
    q_ref, k_ref, v_ref, sems = rest[-4:]
    rows = q_hbm.shape[0]
    own = pl.ds(0, rows)
    copies = [
        pltpu.make_async_copy(q_hbm, q_ref, sems.at[0]),
        pltpu.make_async_copy(k_hbm, k_ref.at[own], sems.at[1]),
        pltpu.make_async_copy(v_hbm, v_ref.at[own], sems.at[2]),
    ]
    for e, edge in enumerate(edges):
        part = pl.ds(rows + e * TILE, TILE)
        copies.append(pltpu.make_async_copy(edge.at[0], k_ref.at[part], sems.at[3 + 2 * e]))
        copies.append(pltpu.make_async_copy(edge.at[1], v_ref.at[part], sems.at[4 + 2 * e]))
    for copy in copies:
        copy.start()
    for copy in copies:
        copy.wait()


def attention_kernel(
    full_width, depth, slot_ref, step_ref, sums_ref, edge_sums_ref, gq_ref, gk_ref, q_ref, k_ref, v_ref,
    out_hbm, out_buf, scale_buf, sems,
):
    tiles, slots = slot_ref.shape
    heads = q_ref.shape[1] // DH
    expert = jnp.where(step_ref[0] >= SWITCH_STEP, 0, 1)
    gain = gq_ref[pl.ds(expert, 1), :] * gk_ref[pl.ds(expert, 1), :] * (DH ** -0.5 * LOG2E)

    def scale(sums):
        return lax.rsqrt(sums * (1.0 / full_width) + EPSILON)

    q_scale = scale(sums_ref[0:tiles, :])
    q_scale = jnp.concatenate([q_scale, jnp.zeros((8 - tiles % 8, TILE), jnp.float32)], axis=0).T
    scale_buf[0:tiles, :] = scale(sums_ref[tiles : 2 * tiles, :])
    scale_buf[tiles : tiles + edge_sums_ref.shape[0], :] = scale(edge_sums_ref[...])
    ones = jnp.ones((TILE, DH), jnp.bfloat16)

    def scores(i, h):
        cols = slice(h * DH, (h + 1) * DH)
        query = q_ref[i * TILE : (i + 1) * TILE, cols].astype(jnp.float32)
        query = (query * q_scale[:, i : i + 1] * gain[:, cols]).astype(jnp.bfloat16)
        return [
            lax.dot_general(
                query, k_ref[tile_rows(slot_ref[i, n]), cols], (((1,), (1,)), ((), ())),
                preferred_element_type=jnp.float32,
            )
            for n in range(slots)
        ]

    def mix(i, h, score):
        cols = slice(h * DH, (h + 1) * DH)
        score = [x * scale_buf[pl.ds(slot_ref[i, n], 1), :] for n, x in enumerate(score)]
        top = jnp.max(functools.reduce(jnp.maximum, score), axis=1, keepdims=True)
        weight = jnp.concatenate([jnp.exp2(x - top).astype(jnp.bfloat16) for x in score], axis=1)
        value = jnp.concatenate(
            [
                jnp.concatenate([v_ref[tile_rows(slot_ref[i, n]), cols], ones], axis=1)
                for n in range(slots)
            ],
            axis=0,
        )
        return jnp.dot(weight, value, preferred_element_type=jnp.float32)

    def finish(i, h, mixed):
        rows = pl.ds(i * TILE, TILE)
        out_buf[rows, h * DH : (h + 1) * DH] = (mixed[:, :DH] / mixed[:, DH:]).astype(jnp.bfloat16)
        if h == heads - 1:
            pltpu.make_async_copy(out_buf.at[rows], out_hbm.at[rows], sems.at[i]).start()

    pairs = [(i, h) for i in range(tiles) for h in range(heads)]
    score, mixed = {}, {}
    for s in range(len(pairs) + depth + 1):
        if s < len(pairs):
            score[s] = scores(*pairs[s])
        if depth <= s < len(pairs) + depth:
            mixed[s - depth] = mix(*pairs[s - depth], score.pop(s - depth))
        if s > depth:
            finish(*pairs[s - depth - 1], mixed.pop(s - depth - 1))
    for i in range(tiles):
        rows = pl.ds(i * TILE, TILE)
        pltpu.make_async_copy(out_buf.at[rows], out_hbm.at[rows], sems.at[i]).wait()


def shards(queries, key_input, value_input, timestep, neighbours, q_gain, k_gain):
    q_rows, k_rows, v_rows = queries[0], key_input[0], value_input[0]
    rows, width = q_rows.shape
    tiles = rows // TILE
    slots = neighbours.shape[2]
    groups, devices = lax.axis_size("mp"), lax.axis_size("seq")
    place = lax.axis_index("seq")

    up = [(i, (i + 1) % devices) for i in range(devices)]
    down = [(i, (i - 1) % devices) for i in range(devices)]
    if devices == 2:
        hops = [up]
        edge_tiles = jnp.where(place == 0, tiles - 1, 0).reshape(1)
    else:
        hops = [down, up]
        edge_tiles = jnp.array([0, tiles - 1], jnp.int32)
    count = len(hops)
    edge_tiles = edge_tiles.astype(jnp.int32)

    chunk = 2 * TILE if tiles % 2 == 0 else TILE
    sums, *edges = pl.pallas_call(
        functools.partial(sums_kernel, chunk),
        out_shape=[pltpu.VMEM((2 * tiles, TILE), jnp.float32)]
        + [pltpu.VMEM((2, TILE, width), jnp.bfloat16)] * count,
        in_specs=[SMEM, HBM, HBM, HBM],
        out_specs=[VMEM] * (1 + count),
        scratch_shapes=[
            pltpu.VMEM((rows, width), jnp.bfloat16),
            pltpu.VMEM((rows, width), jnp.bfloat16),
            pltpu.SemaphoreType.DMA((2, rows // chunk)),
            pltpu.SemaphoreType.DMA((count, 2)),
        ],
        compiler_params=pltpu.CompilerParams(vmem_limit_bytes=58 * MIB),
        cost_estimate=pl.CostEstimate(flops=4 * rows * width, bytes_accessed=4 * rows * width, transcendentals=0),
        name="sums",
    )(edge_tiles, q_rows, k_rows, v_rows)

    total = sums
    for s in list(range(groups - 1, groups - 2, -1)) + list(range(1, groups - 1)):
        total = total + lax.ppermute(sums, "mp", [(i, (i + s) % groups) for i in range(groups)])
    edges = [lax.ppermute(edge, "seq", hop) for edge, hop in zip(edges, hops)]
    edge_sums = jnp.concatenate(
        [
            lax.ppermute(lax.dynamic_slice_in_dim(total, tiles + edge_tiles[e], 1), "seq", hop)
            for e, hop in enumerate(hops)
        ],
        axis=0,
    )

    q_all, k_all, v_all = pl.pallas_call(
        gather_kernel,
        out_shape=[
            pltpu.VMEM((rows, width), jnp.bfloat16),
            pltpu.VMEM((rows + count * TILE, width), jnp.bfloat16),
            pltpu.VMEM((rows + count * TILE, width), jnp.bfloat16),
        ],
        in_specs=[HBM] * 3 + [VMEM] * count,
        out_specs=[VMEM] * 3,
        scratch_shapes=[pltpu.SemaphoreType.DMA((3 + 2 * count,))],
        compiler_params=pltpu.CompilerParams(vmem_limit_bytes=58 * MIB),
        cost_estimate=pl.CostEstimate(flops=0, bytes_accessed=6 * rows * width, transcendentals=0),
        name="gather",
    )(q_rows, k_rows, v_rows, *edges)

    local = neighbours[0] - place * tiles
    where_at = jnp.where(local == tiles, tiles, jnp.where(local < 0, tiles + count - 1, local)).astype(jnp.int32)

    pairs = tiles * slots * TILE * TILE * (width // DH)
    mixed = pl.pallas_call(
        functools.partial(attention_kernel, width * groups, 2),
        out_shape=jax.ShapeDtypeStruct((rows, width), jnp.bfloat16),
        in_specs=[SMEM, SMEM] + [VMEM] * 7,
        out_specs=HBM,
        scratch_shapes=[
            pltpu.VMEM((rows, width), jnp.bfloat16),
            pltpu.VMEM((tiles + 2, TILE), jnp.float32),
            pltpu.SemaphoreType.DMA((tiles,)),
        ],
        compiler_params=pltpu.CompilerParams(vmem_limit_bytes=32 * MIB),
        cost_estimate=pl.CostEstimate(flops=4 * pairs * DH, bytes_accessed=2 * rows * width, transcendentals=pairs),
        name="attention",
    )(where_at, timestep, total, edge_sums, q_gain, k_gain, q_all, k_all, v_all)
    return mixed.reshape(1, rows, width)


def solution(mesh):
    return jax.shard_map(
        shards,
        mesh=mesh,
        in_specs=(
            P("expert", "seq", "mp"),
            P("expert", "seq", "mp"),
            P("expert", "seq", "mp"),
            P("expert"),
            P("expert", "seq", None),
            P(None, "mp"),
            P(None, "mp"),
        ),
        out_specs=P("expert", "seq", "mp"),
        check_vma=False,
    )
```

```python
import functools

import jax
import jax.numpy as jnp
from jax import lax
from jax.experimental import pallas as pl
from jax.experimental.pallas import tpu as pltpu
from jax.sharding import PartitionSpec as P

DH = 128
TILE = 128
EPSILON = 1e-06
SWITCH_STEP = 875
LOG2E = 1.4426950408889634
MIB = 1 << 20

HBM = pl.BlockSpec(memory_space=pltpu.HBM)
VMEM = pl.BlockSpec(memory_space=pltpu.VMEM)
SMEM = pl.BlockSpec(memory_space=pltpu.SMEM)


def tile_rows(index):
    if isinstance(index, int):
        return pl.ds(index * TILE, TILE)
    return pl.ds(pl.multiple_of(index * TILE, TILE), TILE)


def sums_kernel(chunk, edge_ref, q_hbm, k_hbm, v_hbm, sums_ref, q_buf, k_buf, *rest):
    *edges, sems, edge_sems = rest
    rows, width = q_hbm.shape
    copies = []
    for a, (src, dst) in enumerate(((q_hbm, q_buf), (k_hbm, k_buf))):
        for j in range(rows // chunk):
            part = pl.ds(j * chunk, chunk)
            copies.append(pltpu.make_async_copy(src.at[part], dst.at[part], sems.at[a, j]))
            copies[-1].start()
    edge_copies = []
    for e, edge in enumerate(edges):
        part = tile_rows(edge_ref[e])
        for a, src in enumerate((k_hbm, v_hbm)):
            edge_copies.append(pltpu.make_async_copy(src.at[part], edge.at[a], edge_sems.at[e, a]))
            edge_copies[-1].start()
    diagonal = lax.broadcasted_iota(jnp.int32, (TILE, TILE), 0) == lax.broadcasted_iota(
        jnp.int32, (TILE, TILE), 1
    )
    tiles = rows // TILE
    for a, buf in enumerate((q_buf, k_buf)):
        for t in range(tiles):
            if t * TILE % chunk == 0:
                copies[a * (rows // chunk) + t * TILE // chunk].wait()
            total = 0.0
            for j in range(width // DH):
                x = buf[t * TILE : (t + 1) * TILE, j * DH : (j + 1) * DH].astype(jnp.float32)
                total = total + x * x
            total = jnp.sum(total, axis=1, keepdims=True)
            total = jnp.sum(jnp.where(diagonal, total, 0.0), axis=0, keepdims=True)
            sums_ref[a * tiles + t : a * tiles + t + 1, :] = total
    for copy in edge_copies:
        copy.wait()


def scores_kernel(place_ref, step_ref, gq_ref, gk_ref, q_ref, k_ref, v_hbm, *rest):
    del place_ref
    edges = rest[:-3]
    score_ref, v_ref, sems = rest[-3:]
    rows = q_ref.shape[0]
    heads = q_ref.shape[1] // DH
    copies = [pltpu.make_async_copy(v_hbm, v_ref.at[pl.ds(0, rows)], sems.at[0])]
    for e, edge in enumerate(edges):
        part = pl.ds(rows + e * TILE, TILE)
        copies.append(pltpu.make_async_copy(edge.at[1], v_ref.at[part], sems.at[1 + e]))
    for copy in copies:
        copy.start()
    expert = jnp.where(step_ref[0] >= SWITCH_STEP, 0, 1)
    gain = gq_ref[pl.ds(expert, 1), :] * gk_ref[pl.ds(expert, 1), :] * (DH ** -0.5 * LOG2E)
    for h in range(heads):
        cols = slice(h * DH, (h + 1) * DH)
        query = (q_ref[:, cols].astype(jnp.float32) * gain[:, cols]).astype(jnp.bfloat16)
        keys = [k_ref[:, cols]] + [edge[0, :, cols] for edge in edges]
        at = 0
        for key in keys:
            for j in range(0, key.shape[0], 2 * TILE):
                part = key[j : min(j + 2 * TILE, key.shape[0])]
                score_ref[h, :, at : at + part.shape[0]] = lax.dot_general(
                    query, part, (((1,), (1,)), ((), ())), preferred_element_type=jnp.float32
                )
                at += part.shape[0]
    for copy in copies:
        copy.wait()


def attention_kernel(
    full_width, depth, slot_ref, sums_ref, score_ref, v_ref, *rest
):
    *edge_sums, out_hbm, out_buf, k_scale, sems = rest
    tiles, slots = slot_ref.shape[0] - 1, slot_ref.shape[1]
    heads = score_ref.shape[0]

    def scale(sums):
        return lax.rsqrt(sums * (1.0 / full_width) + EPSILON)

    q_scale = scale(sums_ref[0:tiles, :])
    q_scale = jnp.concatenate([q_scale, jnp.zeros((8 - tiles % 8, TILE), jnp.float32)], axis=0).T
    k_scale[0:tiles, :] = scale(sums_ref[tiles : 2 * tiles, :])
    for e, border in enumerate(edge_sums):
        k_scale[tiles + e : tiles + e + 1, :] = scale(border[pl.ds(slot_ref[tiles, e], 1), :])
    ones = jnp.ones((TILE, DH), jnp.bfloat16)

    def weights(i, h):
        rows = pl.ds(i * TILE, TILE)
        score = [
            score_ref[h, rows, tile_rows(slot_ref[i, n])] * k_scale[pl.ds(slot_ref[i, n], 1), :]
            for n in range(slots)
        ]
        top = jnp.max(functools.reduce(jnp.maximum, score), axis=1, keepdims=True)
        return jnp.concatenate(
            [jnp.exp2((x - top) * q_scale[:, i : i + 1]).astype(jnp.bfloat16) for x in score], axis=1
        )

    def mix(i, h, weight):
        cols = slice(h * DH, (h + 1) * DH)
        value = jnp.concatenate(
            [
                jnp.concatenate([v_ref[tile_rows(slot_ref[i, n]), cols], ones], axis=1)
                for n in range(slots)
            ],
            axis=0,
        )
        return jnp.dot(weight, value, preferred_element_type=jnp.float32)

    def finish(i, h, mixed):
        rows = pl.ds(i * TILE, TILE)
        out_buf[rows, h * DH : (h + 1) * DH] = (mixed[:, :DH] / mixed[:, DH:]).astype(jnp.bfloat16)
        if h == heads - 1:
            pltpu.make_async_copy(out_buf.at[rows], out_hbm.at[rows], sems.at[i]).start()

    pairs = [(i, h) for i in range(tiles) for h in range(heads)]
    weight, mixed = {}, {}
    for s in range(len(pairs) + 2 * depth):
        if s < len(pairs):
            weight[s] = weights(*pairs[s])
        if depth <= s < len(pairs) + depth:
            mixed[s - depth] = mix(*pairs[s - depth], weight.pop(s - depth))
        if s >= 2 * depth:
            finish(*pairs[s - 2 * depth], mixed.pop(s - 2 * depth))
    for i in range(tiles):
        rows = pl.ds(i * TILE, TILE)
        pltpu.make_async_copy(out_buf.at[rows], out_hbm.at[rows], sems.at[i]).wait()


def shards(queries, key_input, value_input, timestep, neighbours, q_gain, k_gain):
    q_rows, k_rows, v_rows = queries[0], key_input[0], value_input[0]
    rows, width = q_rows.shape
    tiles = rows // TILE
    slots = neighbours.shape[2]
    groups, devices = lax.axis_size("mp"), lax.axis_size("seq")
    place = lax.axis_index("seq")

    up = [(i, (i + 1) % devices) for i in range(devices)]
    down = [(i, (i - 1) % devices) for i in range(devices)]
    if devices == 2:
        hops = [up]
        edge_tiles = jnp.where(place == 0, tiles - 1, 0).reshape(1)
    else:
        hops = [down, up]
        edge_tiles = jnp.array([0, tiles - 1], jnp.int32)
    count = len(hops)
    edge_tiles = edge_tiles.astype(jnp.int32)

    chunk = 2 * TILE if tiles % 2 == 0 else TILE
    sums, q_all, k_all, *edges = pl.pallas_call(
        functools.partial(sums_kernel, chunk),
        out_shape=[pltpu.VMEM((2 * tiles, TILE), jnp.float32)]
        + [pltpu.VMEM((rows, width), jnp.bfloat16)] * 2
        + [pltpu.VMEM((2, TILE, width), jnp.bfloat16)] * count,
        in_specs=[SMEM, HBM, HBM, HBM],
        out_specs=[VMEM] * (3 + count),
        scratch_shapes=[
            pltpu.SemaphoreType.DMA((2, rows // chunk)),
            pltpu.SemaphoreType.DMA((count, 2)),
        ],
        compiler_params=pltpu.CompilerParams(vmem_limit_bytes=58 * MIB),
        cost_estimate=pl.CostEstimate(flops=4 * rows * width, bytes_accessed=4 * rows * width, transcendentals=0),
        name="sums",
    )(edge_tiles, q_rows, k_rows, v_rows)

    parts = [
        lax.ppermute(sums, "mp", [(i, (i + s) % groups) for i in range(groups)])
        for s in list(range(groups - 1, groups - 2, -1)) + list(range(1, groups - 1))
    ]
    edges = [lax.ppermute(edge, "seq", hop) for edge, hop in zip(edges, hops)]

    local = neighbours[0] - place * tiles
    where_at = jnp.where(local == tiles, tiles, jnp.where(local < 0, tiles + count - 1, local))
    border = jnp.where(jnp.arange(slots) == 0, place, 1) if count == 1 else jnp.minimum(jnp.arange(slots), 1)
    where_at = jnp.concatenate([where_at, border[None]], axis=0).astype(jnp.int32)

    key_rows = rows + count * TILE
    held = width // DH * rows * key_rows * 4 + (key_rows + 2 * rows + 2 * count * TILE) * width * 2
    scores, v_all = pl.pallas_call(
        scores_kernel,
        out_shape=[
            pltpu.VMEM((width // DH, rows, key_rows), jnp.float32),
            pltpu.VMEM((key_rows, width), jnp.bfloat16),
        ],
        in_specs=[SMEM, SMEM, VMEM, VMEM, VMEM, VMEM, HBM] + [VMEM] * count,
        out_specs=[VMEM] * 2,
        scratch_shapes=[pltpu.SemaphoreType.DMA((1 + count,))],
        compiler_params=pltpu.CompilerParams(vmem_limit_bytes=63 * MIB - held),
        cost_estimate=pl.CostEstimate(flops=2 * rows * key_rows * width, bytes_accessed=6 * rows * width, transcendentals=0),
        name="scores",
    )(where_at, timestep, q_gain, k_gain, q_all, k_all, v_rows, *edges)
    *parts, scores, v_all = lax.optimization_barrier((*parts, scores, v_all))

    total = functools.reduce(jnp.add, parts, sums)
    borders = jnp.concatenate([total[tiles : tiles + 1], total[2 * tiles - 1 : 2 * tiles]], axis=0)
    edge_sums = [lax.ppermute(borders, "seq", hop) for hop in hops]

    pairs = tiles * slots * TILE * TILE * (width // DH)
    mixed = pl.pallas_call(
        functools.partial(attention_kernel, width * groups, 1),
        out_shape=jax.ShapeDtypeStruct((rows, width), jnp.bfloat16),
        in_specs=[SMEM] + [VMEM] * (3 + count),
        out_specs=HBM,
        scratch_shapes=[
            pltpu.VMEM((rows, width), jnp.bfloat16),
            pltpu.VMEM((tiles + 2, TILE), jnp.float32),
            pltpu.SemaphoreType.DMA((tiles,)),
        ],
        compiler_params=pltpu.CompilerParams(vmem_limit_bytes=32 * MIB),
        cost_estimate=pl.CostEstimate(flops=2 * pairs * DH, bytes_accessed=2 * rows * width, transcendentals=pairs),
        name="attention",
    )(where_at, total, scores, v_all, *edge_sums)
    return mixed.reshape(1, rows, width)


def solution(mesh):
    return jax.shard_map(
        shards,
        mesh=mesh,
        in_specs=(
            P("expert", "seq", "mp"),
            P("expert", "seq", "mp"),
            P("expert", "seq", "mp"),
            P("expert"),
            P("expert", "seq", None),
            P(None, "mp"),
            P(None, "mp"),
        ),
        out_specs=P("expert", "seq", "mp"),
        check_vma=False,
    )
```

```python
import functools

import jax
import jax.numpy as jnp
from jax import lax
from jax.experimental import pallas as pl
from jax.experimental.pallas import tpu as pltpu
from jax.sharding import PartitionSpec as P

DH = 128
TILE = 128
EPSILON = 1e-06
SWITCH_STEP = 875
LOG2E = 1.4426950408889634
MIB = 1 << 20

HBM = pl.BlockSpec(memory_space=pltpu.HBM)
VMEM = pl.BlockSpec(memory_space=pltpu.VMEM)
SMEM = pl.BlockSpec(memory_space=pltpu.SMEM)


def tile_rows(index):
    if isinstance(index, int):
        return pl.ds(index * TILE, TILE)
    return pl.ds(pl.multiple_of(index * TILE, TILE), TILE)


def sums_kernel(chunk, near_hbm, gq_hbm, gk_hbm, q_hbm, k_hbm, v_hbm, sums_ref, gain_ref, slot_ref,
                q_ref, k_ref, *rest):
    *edges, near, gq, gk, sems, edge_sems, small_sems = rest
    rows, width = q_hbm.shape
    tiles, slots = rows // TILE, near_hbm.shape[0]
    place = lax.axis_index("seq")
    copies = []
    for a, (src, dst) in enumerate(((q_hbm, q_ref), (k_hbm, k_ref))):
        for j in range(rows // chunk):
            part = pl.ds(j * chunk, chunk)
            copies.append(pltpu.make_async_copy(src.at[part], dst.at[part], sems.at[a, j]))
            copies[-1].start()
    small = [
        pltpu.make_async_copy(src, dst, small_sems.at[a])
        for a, (src, dst) in enumerate(((near_hbm, near), (gq_hbm, gq), (gk_hbm, gk)))
    ]
    for copy in small:
        copy.start()
    edge_copies = []
    for e, edge in enumerate(edges):
        first = jnp.where(place == 0, tiles - 1, 0) if len(edges) == 1 else (0, tiles - 1)[e]
        for a, src in enumerate((k_hbm, v_hbm)):
            edge_copies.append(pltpu.make_async_copy(src.at[tile_rows(first)], edge.at[a], edge_sems.at[e, a]))
            edge_copies[-1].start()
    diagonal = lax.broadcasted_iota(jnp.int32, (TILE, TILE), 0) == lax.broadcasted_iota(
        jnp.int32, (TILE, TILE), 1
    )
    for a, buf in enumerate((q_ref, k_ref)):
        for t in range(tiles):
            if t * TILE % chunk == 0:
                copies[a * (rows // chunk) + t * TILE // chunk].wait()
            total = 0.0
            for j in range(width // DH):
                x = buf[t * TILE : (t + 1) * TILE, j * DH : (j + 1) * DH].astype(jnp.float32)
                total = total + x * x
            total = jnp.sum(total, axis=1, keepdims=True)
            total = jnp.sum(jnp.where(diagonal, total, 0.0), axis=0, keepdims=True)
            sums_ref[a * tiles + t : a * tiles + t + 1, :] = total
        if a == 0:
            for copy in small:
                copy.wait()
            gain_ref[...] = gq[...] * gk[...] * (DH ** -0.5 * LOG2E)
            for i in range(tiles):
                for n in range(slots):
                    local = near[n, 0, i] - place * tiles
                    local = jnp.where(local < 0, tiles + len(edges) - 1, jnp.minimum(local, tiles))
                    slot_ref[i * slots + n : i * slots + n + 1, :] = jnp.full((1, TILE), local, jnp.int32)
    for copy in edge_copies:
        copy.wait()


def add_kernel(a_ref, b_ref, out_ref):
    out_ref[...] = a_ref[...] + b_ref[...]


def total_kernel(a_ref, b_ref, out_ref, border_ref):
    total = a_ref[...] + b_ref[...]
    out_ref[...] = total
    tiles = total.shape[0] // 2
    border_ref[0:1, :] = total[tiles : tiles + 1]
    border_ref[1:2, :] = total[2 * tiles - 1 : 2 * tiles]


def expert_gain(step_ref, gain_ref):
    return jnp.where(step_ref[...] >= SWITCH_STEP, gain_ref[0:1, :], gain_ref[1:2, :])


def own_scores(gain, q_ref, k_ref, score_ref, at, h):
    cols = slice(h * DH, (h + 1) * DH)
    query = (q_ref[:, cols].astype(jnp.float32) * gain[:, cols]).astype(jnp.bfloat16)
    rows = k_ref.shape[0]
    for j in range(0, rows, 2 * TILE):
        end = min(j + 2 * TILE, rows)
        score_ref[at, :, j:end] = lax.dot_general(
            query, k_ref[j:end, cols], (((1,), (1,)), ((), ())), preferred_element_type=jnp.float32
        )


def first_kernel(step_ref, gain_ref, q_ref, k_ref, score_ref):
    gain = expert_gain(step_ref, gain_ref)
    for h in range(score_ref.shape[0]):
        own_scores(gain, q_ref, k_ref, score_ref, h, h)


def second_kernel(half_ref, step_ref, gain_ref, q_ref, k_ref, v_hbm, *rest):
    del half_ref
    *edges, given_ref, first_ref, score_ref, v_ref, sems = rest
    del given_ref
    rows = q_ref.shape[0]
    copies = [pltpu.make_async_copy(v_hbm, v_ref.at[pl.ds(0, rows)], sems.at[0])]
    for e, edge in enumerate(edges):
        part = pl.ds(rows + e * TILE, TILE)
        copies.append(pltpu.make_async_copy(edge.at[1], v_ref.at[part], sems.at[1 + e]))
    for copy in copies:
        copy.start()
    gain = expert_gain(step_ref, gain_ref)
    done = first_ref.shape[0]
    for h in range(done + score_ref.shape[0]):
        cols = slice(h * DH, (h + 1) * DH)
        out_ref, at = (first_ref, h) if h < done else (score_ref, h - done)
        if h >= done:
            own_scores(gain, q_ref, k_ref, score_ref, at, h)
        query = (q_ref[:, cols].astype(jnp.float32) * gain[:, cols]).astype(jnp.bfloat16)
        for e, edge in enumerate(edges):
            out_ref[at, :, rows + e * TILE : rows + (e + 1) * TILE] = lax.dot_general(
                query, edge[0, :, cols], (((1,), (1,)), ((), ())), preferred_element_type=jnp.float32
            )
    for copy in copies:
        copy.wait()


def attention_kernel(full_width, block, sums_ref, slot_ref, first_ref, second_ref, v_ref, *rest):
    *borders, out_hbm, out_buf, weight_buf, scale_buf, sems = rest
    tiles = sums_ref.shape[0] // 2
    slots = slot_ref.shape[0] // tiles
    done = first_ref.shape[0]
    heads = done + second_ref.shape[0]
    place = lax.axis_index("seq")

    def scale(sums):
        return lax.rsqrt(sums * (1.0 / full_width) + EPSILON)

    q_scale = scale(sums_ref[0:tiles, :])
    q_scale = jnp.concatenate([q_scale, jnp.zeros((8 - tiles % 8, TILE), jnp.float32)], axis=0).T
    k_scale = [sums_ref[tiles + t : tiles + t + 1, :] for t in range(tiles)]
    if len(borders) == 1:
        k_scale.append(jnp.where(place == 0, borders[0][0:1, :], borders[0][1:2, :]))
    else:
        k_scale += [borders[0][0:1, :], borders[1][1:2, :]]
    listed = slot_ref[...]
    scales = jnp.zeros(listed.shape, jnp.float32)
    for t, row in enumerate(k_scale):
        scales = jnp.where(listed == t, scale(row), scales)
    scale_buf[...] = scales
    slot = [[jnp.max(slot_ref[i * slots + n : i * slots + n + 1, :]) for n in range(slots)] for i in range(tiles)]
    ones = jnp.ones((TILE, DH), jnp.bfloat16)
    buffers = weight_buf.shape[0]

    def weights(s, i, h):
        score_ref, at = (first_ref, h) if h < done else (second_ref, h - done)
        for b in range(TILE // block):
            rows = pl.ds(i * TILE + b * block, block)
            score = [
                score_ref[at, rows, tile_rows(slot[i][n])] * scale_buf[i * slots + n : i * slots + n + 1, :]
                for n in range(slots)
            ]
            top = jnp.max(functools.reduce(jnp.maximum, score), axis=1, keepdims=True)
            for n, x in enumerate(score):
                weight_buf[s % buffers, b * block : (b + 1) * block, n * TILE : (n + 1) * TILE] = jnp.exp2(
                    (x - top) * q_scale[b * block : (b + 1) * block, i : i + 1]
                ).astype(jnp.bfloat16)

    def mix(s, i, h):
        cols = slice(h * DH, (h + 1) * DH)
        value = jnp.concatenate(
            [jnp.concatenate([v_ref[tile_rows(slot[i][n]), cols], ones], axis=1) for n in range(slots)],
            axis=0,
        )
        return jnp.dot(weight_buf[s % buffers], value, preferred_element_type=jnp.float32)

    def finish(i, h, mixed):
        rows = pl.ds(i * TILE, TILE)
        out_buf[rows, h * DH : (h + 1) * DH] = (mixed[:, :DH] / mixed[:, DH:]).astype(jnp.bfloat16)
        if h == heads - 1:
            pltpu.make_async_copy(out_buf.at[rows], out_hbm.at[rows], sems.at[i]).start()

    pairs = [(i, h) for i in range(tiles) for h in range(heads)]
    mixed = {}
    for s in range(len(pairs) + 2):
        if s < len(pairs):
            weights(s, *pairs[s])
        if 1 <= s <= len(pairs):
            mixed[s - 1] = mix(s - 1, *pairs[s - 1])
        if s >= 2:
            finish(*pairs[s - 2], mixed.pop(s - 2))
    for i in range(tiles):
        rows = pl.ds(i * TILE, TILE)
        pltpu.make_async_copy(out_buf.at[rows], out_hbm.at[rows], sems.at[i]).wait()


def shards(queries, key_input, value_input, timestep, neighbours, q_gain, k_gain):
    q_rows, k_rows, v_rows = queries[0], key_input[0], value_input[0]
    rows, width = q_rows.shape
    tiles, heads = rows // TILE, width // DH
    slots = neighbours.shape[2]
    groups, devices = lax.axis_size("mp"), lax.axis_size("seq")

    up = [(i, (i + 1) % devices) for i in range(devices)]
    down = [(i, (i - 1) % devices) for i in range(devices)]
    hops = [up] if devices == 2 else [down, up]
    count = len(hops)

    chunk = 2 * TILE if tiles % 2 == 0 else TILE
    bf16, f32 = jnp.bfloat16, jnp.float32
    sums, gain, slot, q_all, k_all, *edges = pl.pallas_call(
        functools.partial(sums_kernel, chunk),
        out_shape=[
            pltpu.VMEM((2 * tiles, TILE), f32),
            pltpu.VMEM((2, width), f32),
            pltpu.VMEM((tiles * slots, TILE), jnp.int32),
            pltpu.VMEM((rows, width), bf16),
            pltpu.VMEM((rows, width), bf16),
        ]
        + [pltpu.VMEM((2, TILE, width), bf16)] * count,
        in_specs=[HBM] * 6,
        out_specs=[VMEM] * (5 + count),
        scratch_shapes=[
            pltpu.SMEM((slots, 1, tiles), jnp.int32),
            pltpu.VMEM((2, width), f32),
            pltpu.VMEM((2, width), f32),
            pltpu.SemaphoreType.DMA((2, rows // chunk)),
            pltpu.SemaphoreType.DMA((count, 2)),
            pltpu.SemaphoreType.DMA((3,)),
        ],
        compiler_params=pltpu.CompilerParams(vmem_limit_bytes=61 * MIB),
        cost_estimate=pl.CostEstimate(flops=4 * rows * width, bytes_accessed=4 * rows * width, transcendentals=0),
        name="sums",
    )(jnp.transpose(neighbours, (2, 0, 1)), q_gain, k_gain, q_rows, k_rows, v_rows)

    small = pltpu.CompilerParams(vmem_limit_bytes=1 * MIB)
    add = pl.pallas_call(
        add_kernel, out_shape=pltpu.VMEM((2 * tiles, TILE), f32), in_specs=[VMEM] * 2, out_specs=VMEM,
        compiler_params=small, name="add",
    )
    received = lax.ppermute(sums, "mp", [(i, i ^ 1) for i in range(groups)])
    edges = [lax.ppermute(edge, "seq", hop) for edge, hop in zip(edges, hops)]

    key_rows = rows + count * TILE
    early = (heads + 1) // 2
    step = timestep.reshape(1, 1)
    first = pl.pallas_call(
        first_kernel,
        out_shape=pltpu.VMEM((early, rows, key_rows), f32),
        in_specs=[VMEM] * 4,
        out_specs=VMEM,
        compiler_params=pltpu.CompilerParams(vmem_limit_bytes=8 * MIB),
        cost_estimate=pl.CostEstimate(flops=2 * rows * rows * early * DH, bytes_accessed=0, transcendentals=0),
        name="first",
    )(step, gain, q_all, k_all)
    received, first = lax.optimization_barrier((received, first))
    half = add(sums, received)
    received = lax.ppermute(half, "mp", [(i, i ^ 2) for i in range(groups)])
    first, second, v_all = pl.pallas_call(
        second_kernel,
        out_shape=[
            pltpu.VMEM((early, rows, key_rows), f32),
            pltpu.VMEM((heads - early, rows, key_rows), f32),
            pltpu.VMEM((key_rows, width), bf16),
        ],
        in_specs=[VMEM] * 5 + [HBM] + [VMEM] * (count + 1),
        out_specs=[VMEM] * 3,
        input_output_aliases={6 + count: 0},
        scratch_shapes=[pltpu.SemaphoreType.DMA((1 + count,))],
        compiler_params=pltpu.CompilerParams(vmem_limit_bytes=8 * MIB),
        cost_estimate=pl.CostEstimate(flops=2 * rows * rows * early * DH, bytes_accessed=0, transcendentals=0),
        name="second",
    )(half, step, gain, q_all, k_all, v_rows, *edges, first)
    received, first, second, v_all = lax.optimization_barrier((received, first, second, v_all))
    total, border = pl.pallas_call(
        total_kernel,
        out_shape=[pltpu.VMEM((2 * tiles, TILE), f32), pltpu.VMEM((2, TILE), f32)],
        in_specs=[VMEM] * 2, out_specs=[VMEM] * 2, compiler_params=small, name="total",
    )(half, received)
    borders = [lax.ppermute(border, "seq", hop) for hop in hops]

    pairs = tiles * slots * TILE * TILE * heads
    mixed = pl.pallas_call(
        functools.partial(attention_kernel, width * groups, 32),
        out_shape=jax.ShapeDtypeStruct((rows, width), bf16),
        in_specs=[VMEM] * (5 + count),
        out_specs=HBM,
        scratch_shapes=[
            pltpu.VMEM((rows, width), bf16),
            pltpu.VMEM((3, TILE, slots * TILE), bf16),
            pltpu.VMEM((tiles * slots, TILE), f32),
            pltpu.SemaphoreType.DMA((tiles,)),
        ],
        compiler_params=pltpu.CompilerParams(vmem_limit_bytes=24 * MIB),
        cost_estimate=pl.CostEstimate(flops=2 * pairs * DH, bytes_accessed=2 * rows * width, transcendentals=pairs),
        name="attention",
    )(total, slot, first, second, v_all, *borders)
    return mixed.reshape(1, rows, width)


def solution(mesh):
    return jax.shard_map(
        shards,
        mesh=mesh,
        in_specs=(
            P("expert", "seq", "mp"),
            P("expert", "seq", "mp"),
            P("expert", "seq", "mp"),
            P("expert"),
            P("expert", "seq", None),
            P(None, "mp"),
            P(None, "mp"),
        ),
        out_specs=P("expert", "seq", "mp"),
        check_vma=False,
    )
```

```python
import functools

import jax
import jax.numpy as jnp
from jax import lax
from jax.experimental import pallas as pl
from jax.experimental.pallas import tpu as pltpu
from jax.sharding import PartitionSpec as P

DH = 128
TILE = 128
EPSILON = 1e-06
SWITCH_STEP = 875
LOG2E = 1.4426950408889634
MIB = 1 << 20
DEPTH = 1

HBM = pl.BlockSpec(memory_space=pltpu.HBM)
VMEM = pl.BlockSpec(memory_space=pltpu.VMEM)
SMEM = pl.BlockSpec(memory_space=pltpu.SMEM)


def tile_rows(index):
    if isinstance(index, int):
        return pl.ds(index * TILE, TILE)
    return pl.ds(pl.multiple_of(index * TILE, TILE), TILE)


def sums_kernel(chunk, near_hbm, gq_hbm, gk_hbm, q_hbm, k_hbm, v_hbm, sums_ref, gain_ref, slot_ref,
                q_ref, k_ref, *rest):
    *edges, near, gq, gk, sems, edge_sems, small_sems = rest
    rows, width = q_hbm.shape
    tiles, slots = rows // TILE, near_hbm.shape[0]
    place = lax.axis_index("seq")
    copies = []
    for a, (src, dst) in enumerate(((q_hbm, q_ref), (k_hbm, k_ref))):
        for j in range(rows // chunk):
            part = pl.ds(j * chunk, chunk)
            copies.append(pltpu.make_async_copy(src.at[part], dst.at[part], sems.at[a, j]))
            copies[-1].start()
    small = [
        pltpu.make_async_copy(src, dst, small_sems.at[a])
        for a, (src, dst) in enumerate(((near_hbm, near), (gq_hbm, gq), (gk_hbm, gk)))
    ]
    for copy in small:
        copy.start()
    edge_copies = []
    for e, edge in enumerate(edges):
        first = jnp.where(place == 0, tiles - 1, 0) if len(edges) == 1 else (0, tiles - 1)[e]
        for a, src in enumerate((k_hbm, v_hbm)):
            edge_copies.append(pltpu.make_async_copy(src.at[tile_rows(first)], edge.at[a], edge_sems.at[e, a]))
            edge_copies[-1].start()
    diagonal = lax.broadcasted_iota(jnp.int32, (TILE, TILE), 0) == lax.broadcasted_iota(
        jnp.int32, (TILE, TILE), 1
    )
    for a, buf in enumerate((q_ref, k_ref)):
        for t in range(tiles):
            if t * TILE % chunk == 0:
                copies[a * (rows // chunk) + t * TILE // chunk].wait()
            total = 0.0
            for j in range(width // DH):
                x = buf[t * TILE : (t + 1) * TILE, j * DH : (j + 1) * DH].astype(jnp.float32)
                total = total + x * x
            total = jnp.sum(total, axis=1, keepdims=True)
            total = jnp.sum(jnp.where(diagonal, total, 0.0), axis=0, keepdims=True)
            sums_ref[a * tiles + t : a * tiles + t + 1, :] = total
        if a == 0:
            for copy in small:
                copy.wait()
            gain_ref[...] = gq[...] * gk[...] * (DH ** -0.5 * LOG2E)
            for i in range(tiles):
                for n in range(slots):
                    local = near[n, 0, i] - place * tiles
                    local = jnp.where(local < 0, tiles + len(edges) - 1, jnp.minimum(local, tiles))
                    slot_ref[i * slots + n : i * slots + n + 1, :] = jnp.full((1, TILE), local, jnp.int32)
    for copy in edge_copies:
        copy.wait()


def add_kernel(a_ref, b_ref, out_ref):
    out_ref[...] = a_ref[...] + b_ref[...]


def total_kernel(a_ref, b_ref, out_ref, border_ref):
    total = a_ref[...] + b_ref[...]
    out_ref[...] = total
    tiles = total.shape[0] // 2
    border_ref[0:1, :] = total[tiles : tiles + 1]
    border_ref[1:2, :] = total[2 * tiles - 1 : 2 * tiles]


def expert_gain(step_ref, gain_ref):
    return jnp.where(step_ref[...] >= SWITCH_STEP, gain_ref[0:1, :], gain_ref[1:2, :])


def own_scores(gain, q_ref, k_ref, score_ref, at, h):
    cols = slice(h * DH, (h + 1) * DH)
    query = (q_ref[:, cols].astype(jnp.float32) * gain[:, cols]).astype(jnp.bfloat16)
    rows = k_ref.shape[0]
    for j in range(0, rows, 2 * TILE):
        end = min(j + 2 * TILE, rows)
        score_ref[at, :, j:end] = lax.dot_general(
            query, k_ref[j:end, cols], (((1,), (1,)), ((), ())), preferred_element_type=jnp.float32
        )


def first_kernel(step_ref, gain_ref, q_ref, k_ref, score_ref):
    gain = expert_gain(step_ref, gain_ref)
    for h in range(score_ref.shape[0]):
        own_scores(gain, q_ref, k_ref, score_ref, h, h)


def second_kernel(half_ref, step_ref, gain_ref, q_ref, k_ref, v_hbm, *rest):
    del half_ref
    *edges, given_ref, first_ref, score_ref, v_ref, sems = rest
    del given_ref
    rows = q_ref.shape[0]
    copies = [pltpu.make_async_copy(v_hbm, v_ref.at[pl.ds(0, rows)], sems.at[0])]
    for e, edge in enumerate(edges):
        part = pl.ds(rows + e * TILE, TILE)
        copies.append(pltpu.make_async_copy(edge.at[1], v_ref.at[part], sems.at[1 + e]))
    for copy in copies:
        copy.start()
    gain = expert_gain(step_ref, gain_ref)
    done = first_ref.shape[0]
    for h in range(done + score_ref.shape[0]):
        cols = slice(h * DH, (h + 1) * DH)
        out_ref, at = (first_ref, h) if h < done else (score_ref, h - done)
        if h >= done:
            own_scores(gain, q_ref, k_ref, score_ref, at, h)
        query = (q_ref[:, cols].astype(jnp.float32) * gain[:, cols]).astype(jnp.bfloat16)
        for e, edge in enumerate(edges):
            out_ref[at, :, rows + e * TILE : rows + (e + 1) * TILE] = lax.dot_general(
                query, edge[0, :, cols], (((1,), (1,)), ((), ())), preferred_element_type=jnp.float32
            )
    for copy in copies:
        copy.wait()


def attention_kernel(full_width, block, sums_ref, slot_ref, first_ref, second_ref, v_ref, *rest):
    *borders, out_hbm, out_buf, scale_buf, key_buf, sems = rest
    tiles = sums_ref.shape[0] // 2
    slots = slot_ref.shape[0] // tiles
    done = first_ref.shape[0]
    heads = done + second_ref.shape[0]
    place = lax.axis_index("seq")

    def scale(sums):
        return lax.rsqrt(sums * (1.0 / full_width) + EPSILON)

    q_scale = scale(sums_ref[0:tiles, :])
    q_scale = jnp.concatenate([q_scale, jnp.zeros((8 - tiles % 8, TILE), jnp.float32)], axis=0).T
    k_scale = [sums_ref[tiles + t : tiles + t + 1, :] for t in range(tiles)]
    if len(borders) == 1:
        k_scale.append(jnp.where(place == 0, borders[0][0:1, :], borders[0][1:2, :]))
    else:
        k_scale += [borders[0][0:1, :], borders[1][1:2, :]]
    listed = slot_ref[...]
    scales = jnp.zeros(listed.shape, jnp.float32)
    for t, row in enumerate(k_scale):
        scales = jnp.where(listed == t, scale(row), scales)
    key_buf[...] = scales
    slot = [[jnp.max(slot_ref[i * slots + n : i * slots + n + 1, :]) for n in range(slots)] for i in range(tiles)]
    ones = jnp.ones((TILE, DH), jnp.bfloat16)

    def prepare(i):
        for n in range(slots):
            scale_buf[i % 2, :, n * TILE : (n + 1) * TILE] = (
                q_scale[:, i : i + 1] * key_buf[i * slots + n : i * slots + n + 1, :]
            )

    def weights(i, h):
        score_ref, at = (first_ref, h) if h < done else (second_ref, h - done)
        rows = pl.ds(i * TILE, TILE)
        if h == 0:
            prepare(i)
        parts = []
        for b in range(0, TILE, block):
            score = [
                score_ref[at, pl.ds(i * TILE + b, block), tile_rows(slot[i][n])]
                * scale_buf[i % 2, b : b + block, n * TILE : (n + 1) * TILE]
                for n in range(slots)
            ]
            top = jnp.max(functools.reduce(jnp.maximum, score), axis=1, keepdims=True)
            parts.append(jnp.concatenate([jnp.exp2(x - top).astype(jnp.bfloat16) for x in score], axis=1))
        return jnp.concatenate(parts, axis=0)

    def mix(i, h, weight):
        cols = slice(h * DH, (h + 1) * DH)
        value = jnp.concatenate(
            [jnp.concatenate([v_ref[tile_rows(slot[i][n]), cols], ones], axis=1) for n in range(slots)],
            axis=0,
        )
        return jnp.dot(weight, value, preferred_element_type=jnp.float32)

    def finish(i, h, mixed):
        rows = pl.ds(i * TILE, TILE)
        out_buf[rows, h * DH : (h + 1) * DH] = (mixed[:, :DH] / mixed[:, DH:]).astype(jnp.bfloat16)
        if h == heads - 1:
            pltpu.make_async_copy(out_buf.at[rows], out_hbm.at[rows], sems.at[i]).start()

    pairs = [(i, h) for i in range(tiles) for h in range(heads)]
    weight, mixed = {}, {}
    for s in range(len(pairs) + DEPTH + 1):
        if s < len(pairs):
            weight[s] = weights(*pairs[s])
        if DEPTH <= s < len(pairs) + DEPTH:
            mixed[s - DEPTH] = mix(*pairs[s - DEPTH], weight.pop(s - DEPTH))
        if s > DEPTH:
            finish(*pairs[s - DEPTH - 1], mixed.pop(s - DEPTH - 1))
    for i in range(tiles):
        rows = pl.ds(i * TILE, TILE)
        pltpu.make_async_copy(out_buf.at[rows], out_hbm.at[rows], sems.at[i]).wait()


def shards(queries, key_input, value_input, timestep, neighbours, q_gain, k_gain):
    q_rows, k_rows, v_rows = queries[0], key_input[0], value_input[0]
    rows, width = q_rows.shape
    tiles, heads = rows // TILE, width // DH
    slots = neighbours.shape[2]
    groups, devices = lax.axis_size("mp"), lax.axis_size("seq")

    up = [(i, (i + 1) % devices) for i in range(devices)]
    down = [(i, (i - 1) % devices) for i in range(devices)]
    hops = [up] if devices == 2 else [down, up]
    count = len(hops)

    chunk = 2 * TILE if tiles % 2 == 0 else TILE
    bf16, f32 = jnp.bfloat16, jnp.float32
    sums, gain, slot, q_all, k_all, *edges = pl.pallas_call(
        functools.partial(sums_kernel, chunk),
        out_shape=[
            pltpu.VMEM((2 * tiles, TILE), f32),
            pltpu.VMEM((2, width), f32),
            pltpu.VMEM((tiles * slots, TILE), jnp.int32),
            pltpu.VMEM((rows, width), bf16),
            pltpu.VMEM((rows, width), bf16),
        ]
        + [pltpu.VMEM((2, TILE, width), bf16)] * count,
        in_specs=[HBM] * 6,
        out_specs=[VMEM] * (5 + count),
        scratch_shapes=[
            pltpu.SMEM((slots, 1, tiles), jnp.int32),
            pltpu.VMEM((2, width), f32),
            pltpu.VMEM((2, width), f32),
            pltpu.SemaphoreType.DMA((2, rows // chunk)),
            pltpu.SemaphoreType.DMA((count, 2)),
            pltpu.SemaphoreType.DMA((3,)),
        ],
        compiler_params=pltpu.CompilerParams(vmem_limit_bytes=61 * MIB),
        cost_estimate=pl.CostEstimate(flops=4 * rows * width, bytes_accessed=4 * rows * width, transcendentals=0),
        name="sums",
    )(jnp.transpose(neighbours, (2, 0, 1)), q_gain, k_gain, q_rows, k_rows, v_rows)

    small = pltpu.CompilerParams(vmem_limit_bytes=1 * MIB)
    add = pl.pallas_call(
        add_kernel, out_shape=pltpu.VMEM((2 * tiles, TILE), f32), in_specs=[VMEM] * 2, out_specs=VMEM,
        compiler_params=small, name="add",
    )
    received = lax.ppermute(sums, "mp", [(i, i ^ 1) for i in range(groups)])
    edges = [lax.ppermute(edge, "seq", hop) for edge, hop in zip(edges, hops)]

    key_rows = rows + count * TILE
    early = (heads + 1) // 2
    step = timestep.reshape(1, 1)
    first = pl.pallas_call(
        first_kernel,
        out_shape=pltpu.VMEM((early, rows, key_rows), f32),
        in_specs=[VMEM] * 4,
        out_specs=VMEM,
        compiler_params=pltpu.CompilerParams(vmem_limit_bytes=8 * MIB),
        cost_estimate=pl.CostEstimate(flops=2 * rows * rows * early * DH, bytes_accessed=0, transcendentals=0),
        name="first",
    )(step, gain, q_all, k_all)
    received, first = lax.optimization_barrier((received, first))
    half = add(sums, received)
    received = lax.ppermute(half, "mp", [(i, i ^ 2) for i in range(groups)])
    first, second, v_all = pl.pallas_call(
        second_kernel,
        out_shape=[
            pltpu.VMEM((early, rows, key_rows), f32),
            pltpu.VMEM((heads - early, rows, key_rows), f32),
            pltpu.VMEM((key_rows, width), bf16),
        ],
        in_specs=[VMEM] * 5 + [HBM] + [VMEM] * (count + 1),
        out_specs=[VMEM] * 3,
        input_output_aliases={6 + count: 0},
        scratch_shapes=[pltpu.SemaphoreType.DMA((1 + count,))],
        compiler_params=pltpu.CompilerParams(vmem_limit_bytes=8 * MIB),
        cost_estimate=pl.CostEstimate(flops=2 * rows * rows * early * DH, bytes_accessed=0, transcendentals=0),
        name="second",
    )(half, step, gain, q_all, k_all, v_rows, *edges, first)
    received, first, second, v_all = lax.optimization_barrier((received, first, second, v_all))
    total, border = pl.pallas_call(
        total_kernel,
        out_shape=[pltpu.VMEM((2 * tiles, TILE), f32), pltpu.VMEM((2, TILE), f32)],
        in_specs=[VMEM] * 2, out_specs=[VMEM] * 2, compiler_params=small, name="total",
    )(half, received)
    borders = [lax.ppermute(border, "seq", hop) for hop in hops]

    pairs = tiles * slots * TILE * TILE * heads
    mixed = pl.pallas_call(
        functools.partial(attention_kernel, width * groups, 128),
        out_shape=jax.ShapeDtypeStruct((rows, width), bf16),
        in_specs=[VMEM] * (5 + count),
        out_specs=HBM,
        scratch_shapes=[
            pltpu.VMEM((rows, width), bf16),
            pltpu.VMEM((2, TILE, slots * TILE), f32),
            pltpu.VMEM((tiles * slots, TILE), f32),
            pltpu.SemaphoreType.DMA((tiles,)),
        ],
        compiler_params=pltpu.CompilerParams(vmem_limit_bytes=24 * MIB),
        cost_estimate=pl.CostEstimate(flops=2 * pairs * DH, bytes_accessed=2 * rows * width, transcendentals=pairs),
        name="attention",
    )(total, slot, first, second, v_all, *borders)
    return mixed.reshape(1, rows, width)


def solution(mesh):
    return jax.shard_map(
        shards,
        mesh=mesh,
        in_specs=(
            P("expert", "seq", "mp"),
            P("expert", "seq", "mp"),
            P("expert", "seq", "mp"),
            P("expert"),
            P("expert", "seq", None),
            P(None, "mp"),
            P(None, "mp"),
        ),
        out_specs=P("expert", "seq", "mp"),
        check_vma=False,
    )
```

```python
import functools

import jax
import jax.numpy as jnp
from jax import lax
from jax.experimental import pallas as pl
from jax.experimental.pallas import tpu as pltpu
from jax.sharding import PartitionSpec as P

DH = 128
TILE = 128
EPSILON = 1e-06
SWITCH_STEP = 875
LOG2E = 1.4426950408889634
MIB = 1 << 20
DEPTH = 1

HBM = pl.BlockSpec(memory_space=pltpu.HBM)
VMEM = pl.BlockSpec(memory_space=pltpu.VMEM)
SMEM = pl.BlockSpec(memory_space=pltpu.SMEM)


def tile_rows(index):
    if isinstance(index, int):
        return pl.ds(index * TILE, TILE)
    return pl.ds(pl.multiple_of(index * TILE, TILE), TILE)


def sums_kernel(chunk, near_hbm, gq_hbm, gk_hbm, q_hbm, k_hbm, v_hbm, sums_ref, gain_ref, slot_ref,
                q_ref, k_ref, *rest):
    *edges, near, gq, gk, sems, edge_sems, small_sems = rest
    rows, width = q_hbm.shape
    tiles, slots = rows // TILE, near_hbm.shape[0]
    place = lax.axis_index("seq")
    copies = []
    for a, (src, dst) in enumerate(((q_hbm, q_ref), (k_hbm, k_ref))):
        for j in range(rows // chunk):
            part = pl.ds(j * chunk, chunk)
            copies.append(pltpu.make_async_copy(src.at[part], dst.at[part], sems.at[a, j]))
            copies[-1].start()
    small = [
        pltpu.make_async_copy(src, dst, small_sems.at[a])
        for a, (src, dst) in enumerate(((near_hbm, near), (gq_hbm, gq), (gk_hbm, gk)))
    ]
    for copy in small:
        copy.start()
    edge_copies = []
    for e, edge in enumerate(edges):
        first = jnp.where(place == 0, tiles - 1, 0) if len(edges) == 1 else (0, tiles - 1)[e]
        for a, src in enumerate((k_hbm, v_hbm)):
            edge_copies.append(pltpu.make_async_copy(src.at[tile_rows(first)], edge.at[a], edge_sems.at[e, a]))
            edge_copies[-1].start()
    diagonal = lax.broadcasted_iota(jnp.int32, (TILE, TILE), 0) == lax.broadcasted_iota(
        jnp.int32, (TILE, TILE), 1
    )
    for a, buf in enumerate((q_ref, k_ref)):
        for t in range(tiles):
            if t * TILE % chunk == 0:
                copies[a * (rows // chunk) + t * TILE // chunk].wait()
            total = 0.0
            for j in range(width // DH):
                x = buf[t * TILE : (t + 1) * TILE, j * DH : (j + 1) * DH].astype(jnp.float32)
                total = total + x * x
            total = jnp.sum(total, axis=1, keepdims=True)
            total = jnp.sum(jnp.where(diagonal, total, 0.0), axis=0, keepdims=True)
            sums_ref[a * tiles + t : a * tiles + t + 1, :] = total
        if a == 0:
            for copy in small:
                copy.wait()
            gain_ref[...] = gq[...] * gk[...] * (DH ** -0.5 * LOG2E)
            for i in range(tiles):
                for n in range(slots):
                    local = near[n, 0, i] - place * tiles
                    local = jnp.where(local < 0, tiles + len(edges) - 1, jnp.minimum(local, tiles))
                    slot_ref[i * slots + n : i * slots + n + 1, :] = jnp.full((1, TILE), local, jnp.int32)
    for copy in edge_copies:
        copy.wait()


def half_kernel(a_ref, b_ref, out_ref, border_ref):
    half = a_ref[...] + b_ref[...]
    out_ref[...] = half
    tiles = half.shape[0] // 2
    border_ref[0:1, :] = half[tiles : tiles + 1]
    border_ref[1:2, :] = half[2 * tiles - 1 : 2 * tiles]


def expert_gain(step_ref, gain_ref):
    return jnp.where(step_ref[...] >= SWITCH_STEP, gain_ref[0:1, :], gain_ref[1:2, :])


def own_scores(gain, q_ref, k_ref, score_ref, at, h):
    cols = slice(h * DH, (h + 1) * DH)
    query = (q_ref[:, cols].astype(jnp.float32) * gain[:, cols]).astype(jnp.bfloat16)
    rows = k_ref.shape[0]
    for j in range(0, rows, 2 * TILE):
        end = min(j + 2 * TILE, rows)
        score_ref[at, :, j:end] = lax.dot_general(
            query, k_ref[j:end, cols], (((1,), (1,)), ((), ())), preferred_element_type=jnp.float32
        )


def first_kernel(step_ref, gain_ref, q_ref, k_ref, score_ref):
    gain = expert_gain(step_ref, gain_ref)
    for h in range(score_ref.shape[0]):
        own_scores(gain, q_ref, k_ref, score_ref, h, h)


def second_kernel(half_ref, step_ref, gain_ref, q_ref, k_ref, v_hbm, *rest):
    del half_ref
    *edges, given_ref, first_ref, score_ref, v_ref, sems = rest
    del given_ref
    rows = q_ref.shape[0]
    copies = [pltpu.make_async_copy(v_hbm, v_ref.at[pl.ds(0, rows)], sems.at[0])]
    for e, edge in enumerate(edges):
        part = pl.ds(rows + e * TILE, TILE)
        copies.append(pltpu.make_async_copy(edge.at[1], v_ref.at[part], sems.at[1 + e]))
    for copy in copies:
        copy.start()
    gain = expert_gain(step_ref, gain_ref)
    done = first_ref.shape[0]
    for h in range(done + score_ref.shape[0]):
        cols = slice(h * DH, (h + 1) * DH)
        out_ref, at = (first_ref, h) if h < done else (score_ref, h - done)
        if h >= done:
            own_scores(gain, q_ref, k_ref, score_ref, at, h)
        query = (q_ref[:, cols].astype(jnp.float32) * gain[:, cols]).astype(jnp.bfloat16)
        for e, edge in enumerate(edges):
            out_ref[at, :, rows + e * TILE : rows + (e + 1) * TILE] = lax.dot_general(
                query, edge[0, :, cols], (((1,), (1,)), ((), ())), preferred_element_type=jnp.float32
            )
    for copy in copies:
        copy.wait()


def attention_kernel(full_width, block, half_ref, other_ref, slot_ref, first_ref, second_ref, v_ref, *rest):
    *borders, out_hbm, out_buf, scale_buf, key_buf, sems = rest
    borders = [a[...] + b[...] for a, b in zip(borders[: len(borders) // 2], borders[len(borders) // 2 :])]
    sums = half_ref[...] + other_ref[...]
    tiles = sums.shape[0] // 2
    slots = slot_ref.shape[0] // tiles
    done = first_ref.shape[0]
    heads = done + second_ref.shape[0]
    place = lax.axis_index("seq")

    def scale(sums):
        return lax.rsqrt(sums * (1.0 / full_width) + EPSILON)

    q_scale = scale(sums[0:tiles, :])
    q_scale = jnp.concatenate([q_scale, jnp.zeros((8 - tiles % 8, TILE), jnp.float32)], axis=0).T
    k_scale = [sums[tiles + t : tiles + t + 1, :] for t in range(tiles)]
    if len(borders) == 1:
        k_scale.append(jnp.where(place == 0, borders[0][0:1, :], borders[0][1:2, :]))
    else:
        k_scale += [borders[0][0:1, :], borders[1][1:2, :]]
    listed = slot_ref[...]
    scales = jnp.zeros(listed.shape, jnp.float32)
    for t, row in enumerate(k_scale):
        scales = jnp.where(listed == t, scale(row), scales)
    key_buf[...] = scales
    slot = [[jnp.max(slot_ref[i * slots + n : i * slots + n + 1, :]) for n in range(slots)] for i in range(tiles)]
    ones = jnp.ones((TILE, DH), jnp.bfloat16)

    def prepare(i):
        for n in range(slots):
            scale_buf[i % 2, :, n * TILE : (n + 1) * TILE] = (
                q_scale[:, i : i + 1] * key_buf[i * slots + n : i * slots + n + 1, :]
            )

    def weights(i, h):
        score_ref, at = (first_ref, h) if h < done else (second_ref, h - done)
        rows = pl.ds(i * TILE, TILE)
        if h == 0:
            prepare(i)
        parts = []
        for b in range(0, TILE, block):
            score = [
                score_ref[at, pl.ds(i * TILE + b, block), tile_rows(slot[i][n])]
                * scale_buf[i % 2, b : b + block, n * TILE : (n + 1) * TILE]
                for n in range(slots)
            ]
            top = jnp.max(functools.reduce(jnp.maximum, score), axis=1, keepdims=True)
            parts.append(jnp.concatenate([jnp.exp2(x - top).astype(jnp.bfloat16) for x in score], axis=1))
        return jnp.concatenate(parts, axis=0)

    def mix(i, h, weight):
        cols = slice(h * DH, (h + 1) * DH)
        value = jnp.concatenate(
            [jnp.concatenate([v_ref[tile_rows(slot[i][n]), cols], ones], axis=1) for n in range(slots)],
            axis=0,
        )
        return jnp.dot(weight, value, preferred_element_type=jnp.float32)

    def finish(i, h, mixed):
        rows = pl.ds(i * TILE, TILE)
        out_buf[rows, h * DH : (h + 1) * DH] = (mixed[:, :DH] / mixed[:, DH:]).astype(jnp.bfloat16)
        if h == heads - 1:
            pltpu.make_async_copy(out_buf.at[rows], out_hbm.at[rows], sems.at[i]).start()

    pairs = [(i, h) for i in range(tiles) for h in range(heads)]
    weight, mixed = {}, {}
    for s in range(len(pairs) + DEPTH + 1):
        if s < len(pairs):
            weight[s] = weights(*pairs[s])
        if DEPTH <= s < len(pairs) + DEPTH:
            mixed[s - DEPTH] = mix(*pairs[s - DEPTH], weight.pop(s - DEPTH))
        if s > DEPTH:
            finish(*pairs[s - DEPTH - 1], mixed.pop(s - DEPTH - 1))
    for i in range(tiles):
        rows = pl.ds(i * TILE, TILE)
        pltpu.make_async_copy(out_buf.at[rows], out_hbm.at[rows], sems.at[i]).wait()


def shards(queries, key_input, value_input, timestep, neighbours, q_gain, k_gain):
    q_rows, k_rows, v_rows = queries[0], key_input[0], value_input[0]
    rows, width = q_rows.shape
    tiles, heads = rows // TILE, width // DH
    slots = neighbours.shape[2]
    groups, devices = lax.axis_size("mp"), lax.axis_size("seq")

    up = [(i, (i + 1) % devices) for i in range(devices)]
    down = [(i, (i - 1) % devices) for i in range(devices)]
    hops = [up] if devices == 2 else [down, up]
    count = len(hops)

    chunk = 2 * TILE if tiles % 2 == 0 else TILE
    bf16, f32 = jnp.bfloat16, jnp.float32
    sums, gain, slot, q_all, k_all, *edges = pl.pallas_call(
        functools.partial(sums_kernel, chunk),
        out_shape=[
            pltpu.VMEM((2 * tiles, TILE), f32),
            pltpu.VMEM((2, width), f32),
            pltpu.VMEM((tiles * slots, TILE), jnp.int32),
            pltpu.VMEM((rows, width), bf16),
            pltpu.VMEM((rows, width), bf16),
        ]
        + [pltpu.VMEM((2, TILE, width), bf16)] * count,
        in_specs=[HBM] * 6,
        out_specs=[VMEM] * (5 + count),
        scratch_shapes=[
            pltpu.SMEM((slots, 1, tiles), jnp.int32),
            pltpu.VMEM((2, width), f32),
            pltpu.VMEM((2, width), f32),
            pltpu.SemaphoreType.DMA((2, rows // chunk)),
            pltpu.SemaphoreType.DMA((count, 2)),
            pltpu.SemaphoreType.DMA((3,)),
        ],
        compiler_params=pltpu.CompilerParams(vmem_limit_bytes=61 * MIB),
        cost_estimate=pl.CostEstimate(flops=4 * rows * width, bytes_accessed=4 * rows * width, transcendentals=0),
        name="sums",
    )(jnp.transpose(neighbours, (2, 0, 1)), q_gain, k_gain, q_rows, k_rows, v_rows)

    small = pltpu.CompilerParams(vmem_limit_bytes=1 * MIB)
    received = lax.ppermute(sums, "mp", [(i, i ^ 1) for i in range(groups)])
    edges = [lax.ppermute(edge, "seq", hop) for edge, hop in zip(edges, hops)]

    key_rows = rows + count * TILE
    early = (heads + 1) // 2
    step = timestep.reshape(1, 1)
    first = pl.pallas_call(
        first_kernel,
        out_shape=pltpu.VMEM((early, rows, key_rows), f32),
        in_specs=[VMEM] * 4,
        out_specs=VMEM,
        compiler_params=pltpu.CompilerParams(vmem_limit_bytes=8 * MIB),
        cost_estimate=pl.CostEstimate(flops=2 * rows * rows * early * DH, bytes_accessed=0, transcendentals=0),
        name="first",
    )(step, gain, q_all, k_all)
    received, first = lax.optimization_barrier((received, first))
    half, border = pl.pallas_call(
        half_kernel,
        out_shape=[pltpu.VMEM((2 * tiles, TILE), f32), pltpu.VMEM((2, TILE), f32)],
        in_specs=[VMEM] * 2, out_specs=[VMEM] * 2, compiler_params=small, name="half",
    )(sums, received)
    received = lax.ppermute(half, "mp", [(i, i ^ 2) for i in range(groups)])
    across = [
        lax.ppermute(
            border, ("seq", "mp"),
            [(a * groups + i, b * groups + (i ^ 2)) for a, b in hop for i in range(groups)],
        )
        for hop in hops
    ]
    beside = [lax.ppermute(border, "seq", hop) for hop in hops]
    first, second, v_all = pl.pallas_call(
        second_kernel,
        out_shape=[
            pltpu.VMEM((early, rows, key_rows), f32),
            pltpu.VMEM((heads - early, rows, key_rows), f32),
            pltpu.VMEM((key_rows, width), bf16),
        ],
        in_specs=[VMEM] * 5 + [HBM] + [VMEM] * (count + 1),
        out_specs=[VMEM] * 3,
        input_output_aliases={6 + count: 0},
        scratch_shapes=[pltpu.SemaphoreType.DMA((1 + count,))],
        compiler_params=pltpu.CompilerParams(vmem_limit_bytes=8 * MIB),
        cost_estimate=pl.CostEstimate(flops=2 * rows * rows * early * DH, bytes_accessed=0, transcendentals=0),
        name="second",
    )(half, step, gain, q_all, k_all, v_rows, *edges, first)
    received, across, beside, first, second, v_all = lax.optimization_barrier(
        (received, across, beside, first, second, v_all)
    )

    pairs = tiles * slots * TILE * TILE * heads
    mixed = pl.pallas_call(
        functools.partial(attention_kernel, width * groups, 128),
        out_shape=jax.ShapeDtypeStruct((rows, width), bf16),
        in_specs=[VMEM] * (6 + 2 * count),
        out_specs=HBM,
        scratch_shapes=[
            pltpu.VMEM((rows, width), bf16),
            pltpu.VMEM((2, TILE, slots * TILE), f32),
            pltpu.VMEM((tiles * slots, TILE), f32),
            pltpu.SemaphoreType.DMA((tiles,)),
        ],
        compiler_params=pltpu.CompilerParams(vmem_limit_bytes=24 * MIB),
        cost_estimate=pl.CostEstimate(flops=2 * pairs * DH, bytes_accessed=2 * rows * width, transcendentals=pairs),
        name="attention",
    )(half, received, slot, first, second, v_all, *across, *beside)
    return mixed.reshape(1, rows, width)


def solution(mesh):
    return jax.shard_map(
        shards,
        mesh=mesh,
        in_specs=(
            P("expert", "seq", "mp"),
            P("expert", "seq", "mp"),
            P("expert", "seq", "mp"),
            P("expert"),
            P("expert", "seq", None),
            P(None, "mp"),
            P(None, "mp"),
        ),
        out_specs=P("expert", "seq", "mp"),
        check_vma=False,
    )
```

```python
import functools

import jax
import jax.numpy as jnp
from jax import lax
from jax.experimental import pallas as pl
from jax.experimental.pallas import tpu as pltpu
from jax.sharding import PartitionSpec as P

DH = 128
TILE = 128
EPSILON = 1e-06
SWITCH_STEP = 875
LOG2E = 1.4426950408889634
MIB = 1 << 20
DEPTH = 1

HBM = pl.BlockSpec(memory_space=pltpu.HBM)
VMEM = pl.BlockSpec(memory_space=pltpu.VMEM)
SMEM = pl.BlockSpec(memory_space=pltpu.SMEM)


def tile_rows(index):
    if isinstance(index, int):
        return pl.ds(index * TILE, TILE)
    return pl.ds(pl.multiple_of(index * TILE, TILE), TILE)


def sums_kernel(chunk, near_hbm, gq_hbm, gk_hbm, q_hbm, k_hbm, v_hbm, sums_ref, gain_ref, slot_ref,
                q_ref, k_ref, *rest):
    *edges, near, gq, gk, sems, edge_sems, small_sems = rest
    rows, width = q_hbm.shape
    tiles, slots = rows // TILE, near_hbm.shape[0]
    place = lax.axis_index("seq")
    copies = []
    for a, (src, dst) in enumerate(((q_hbm, q_ref), (k_hbm, k_ref))):
        for j in range(rows // chunk):
            part = pl.ds(j * chunk, chunk)
            copies.append(pltpu.make_async_copy(src.at[part], dst.at[part], sems.at[a, j]))
            copies[-1].start()
    small = [
        pltpu.make_async_copy(src, dst, small_sems.at[a])
        for a, (src, dst) in enumerate(((near_hbm, near), (gq_hbm, gq), (gk_hbm, gk)))
    ]
    for copy in small:
        copy.start()
    edge_copies = []
    for e, edge in enumerate(edges):
        first = jnp.where(place == 0, tiles - 1, 0) if len(edges) == 1 else (0, tiles - 1)[e]
        for a, src in enumerate((k_hbm, v_hbm)):
            edge_copies.append(pltpu.make_async_copy(src.at[tile_rows(first)], edge.at[a], edge_sems.at[e, a]))
            edge_copies[-1].start()
    diagonal = lax.broadcasted_iota(jnp.int32, (TILE, TILE), 0) == lax.broadcasted_iota(
        jnp.int32, (TILE, TILE), 1
    )
    for a, buf in enumerate((q_ref, k_ref)):
        for t in range(tiles):
            if t * TILE % chunk == 0:
                copies[a * (rows // chunk) + t * TILE // chunk].wait()
            total = 0.0
            for j in range(width // DH):
                x = buf[t * TILE : (t + 1) * TILE, j * DH : (j + 1) * DH].astype(jnp.float32)
                total = total + x * x
            total = jnp.sum(total, axis=1, keepdims=True)
            total = jnp.sum(jnp.where(diagonal, total, 0.0), axis=0, keepdims=True)
            sums_ref[a * tiles + t : a * tiles + t + 1, :] = total
        if a == 0:
            for copy in small:
                copy.wait()
            gain_ref[...] = gq[...] * gk[...] * (DH ** -0.5 * LOG2E)
            for i in range(tiles):
                for n in range(slots):
                    local = near[n, 0, i] - place * tiles
                    local = jnp.where(local < 0, tiles + len(edges) - 1, jnp.minimum(local, tiles))
                    slot_ref[i * slots + n : i * slots + n + 1, :] = jnp.full((1, TILE), local, jnp.int32)
    for copy in edge_copies:
        copy.wait()


def add_kernel(a_ref, b_ref, out_ref):
    out_ref[...] = a_ref[...] + b_ref[...]


def total_kernel(a_ref, b_ref, out_ref, border_ref):
    total = a_ref[...] + b_ref[...]
    out_ref[...] = total
    tiles = total.shape[0] // 2
    border_ref[0:1, :] = total[tiles : tiles + 1]
    border_ref[1:2, :] = total[2 * tiles - 1 : 2 * tiles]


def expert_gain(step_ref, gain_ref):
    return jnp.where(step_ref[...] >= SWITCH_STEP, gain_ref[0:1, :], gain_ref[1:2, :])


def own_scores(gain, q_ref, k_ref, score_ref, at, h):
    cols = slice(h * DH, (h + 1) * DH)
    query = (q_ref[:, cols].astype(jnp.float32) * gain[:, cols]).astype(jnp.bfloat16)
    rows = k_ref.shape[0]
    for j in range(0, rows, 2 * TILE):
        end = min(j + 2 * TILE, rows)
        score_ref[at, :, j:end] = lax.dot_general(
            query, k_ref[j:end, cols], (((1,), (1,)), ((), ())), preferred_element_type=jnp.float32
        )


def first_kernel(step_ref, gain_ref, q_ref, k_ref, score_ref):
    gain = expert_gain(step_ref, gain_ref)
    for h in range(score_ref.shape[0]):
        own_scores(gain, q_ref, k_ref, score_ref, h, h)


def second_kernel(half_ref, step_ref, gain_ref, q_ref, k_ref, v_hbm, *rest):
    del half_ref
    *edges, given_ref, first_ref, score_ref, v_ref, sems = rest
    del given_ref
    rows = q_ref.shape[0]
    copies = [pltpu.make_async_copy(v_hbm, v_ref.at[pl.ds(0, rows)], sems.at[0])]
    for e, edge in enumerate(edges):
        part = pl.ds(rows + e * TILE, TILE)
        copies.append(pltpu.make_async_copy(edge.at[1], v_ref.at[part], sems.at[1 + e]))
    for copy in copies:
        copy.start()
    gain = expert_gain(step_ref, gain_ref)
    done = first_ref.shape[0]
    for h in range(done + score_ref.shape[0]):
        cols = slice(h * DH, (h + 1) * DH)
        out_ref, at = (first_ref, h) if h < done else (score_ref, h - done)
        if h >= done:
            own_scores(gain, q_ref, k_ref, score_ref, at, h)
        query = (q_ref[:, cols].astype(jnp.float32) * gain[:, cols]).astype(jnp.bfloat16)
        for e, edge in enumerate(edges):
            out_ref[at, :, rows + e * TILE : rows + (e + 1) * TILE] = lax.dot_general(
                query, edge[0, :, cols], (((1,), (1,)), ((), ())), preferred_element_type=jnp.float32
            )
    for copy in copies:
        copy.wait()


def scale_kernel(full_width, first_tile, sums_ref, *rest):
    *borders, _, _, first_ref, second_ref = rest
    tiles = sums_ref.shape[0] // 2

    def scale(sums):
        return lax.rsqrt(sums * (1.0 / full_width) + EPSILON)

    if not borders:
        k_scale = [scale(sums_ref[tiles + t : tiles + t + 1, :]) for t in range(tiles)]
    elif len(borders) == 1:
        place = lax.axis_index("seq")
        k_scale = [scale(jnp.where(place == 0, borders[0][0:1, :], borders[0][1:2, :]))]
    else:
        k_scale = [scale(borders[0][0:1, :]), scale(borders[1][1:2, :])]
    q_scale = scale(sums_ref[0:tiles, :])
    q_scale = jnp.concatenate([q_scale, jnp.zeros((8 - tiles % 8, TILE), jnp.float32)], axis=0).T
    for i in range(tiles):
        column = jnp.broadcast_to(q_scale[:, i : i + 1], (TILE, TILE))
        rows = slice(i * TILE, (i + 1) * TILE)
        for t, row in enumerate(k_scale):
            both = column * row
            cols = slice((first_tile + t) * TILE, (first_tile + t + 1) * TILE)
            for ref in (first_ref, second_ref):
                for h in range(ref.shape[0]):
                    ref[h, rows, cols] = ref[h, rows, cols] * both


def attention_kernel(tiles, slot_ref, first_ref, second_ref, v_ref, out_hbm, out_buf, sems):
    slots = slot_ref.shape[0] // tiles
    done = first_ref.shape[0]
    heads = done + second_ref.shape[0]
    slot = [[jnp.max(slot_ref[i * slots + n : i * slots + n + 1, :]) for n in range(slots)] for i in range(tiles)]
    ones = jnp.ones((TILE, DH), jnp.bfloat16)

    def weights(i, h):
        score_ref, at = (first_ref, h) if h < done else (second_ref, h - done)
        rows = pl.ds(i * TILE, TILE)
        score = [score_ref[at, rows, tile_rows(slot[i][n])] for n in range(slots)]
        top = jnp.max(functools.reduce(jnp.maximum, score), axis=1, keepdims=True)
        return jnp.concatenate([jnp.exp2(x - top).astype(jnp.bfloat16) for x in score], axis=1)

    def mix(i, h, weight):
        cols = slice(h * DH, (h + 1) * DH)
        value = jnp.concatenate(
            [jnp.concatenate([v_ref[tile_rows(slot[i][n]), cols], ones], axis=1) for n in range(slots)],
            axis=0,
        )
        return jnp.dot(weight, value, preferred_element_type=jnp.float32)

    def finish(i, h, mixed):
        rows = pl.ds(i * TILE, TILE)
        out_buf[rows, h * DH : (h + 1) * DH] = (mixed[:, :DH] / mixed[:, DH:]).astype(jnp.bfloat16)
        if h == heads - 1:
            pltpu.make_async_copy(out_buf.at[rows], out_hbm.at[rows], sems.at[i]).start()

    pairs = [(i, h) for i in range(tiles) for h in range(heads)]
    weight, mixed = {}, {}
    for s in range(len(pairs) + DEPTH + 1):
        if s < len(pairs):
            weight[s] = weights(*pairs[s])
        if DEPTH <= s < len(pairs) + DEPTH:
            mixed[s - DEPTH] = mix(*pairs[s - DEPTH], weight.pop(s - DEPTH))
        if s > DEPTH:
            finish(*pairs[s - DEPTH - 1], mixed.pop(s - DEPTH - 1))
    for i in range(tiles):
        rows = pl.ds(i * TILE, TILE)
        pltpu.make_async_copy(out_buf.at[rows], out_hbm.at[rows], sems.at[i]).wait()


def shards(queries, key_input, value_input, timestep, neighbours, q_gain, k_gain):
    q_rows, k_rows, v_rows = queries[0], key_input[0], value_input[0]
    rows, width = q_rows.shape
    tiles, heads = rows // TILE, width // DH
    slots = neighbours.shape[2]
    groups, devices = lax.axis_size("mp"), lax.axis_size("seq")

    up = [(i, (i + 1) % devices) for i in range(devices)]
    down = [(i, (i - 1) % devices) for i in range(devices)]
    hops = [up] if devices == 2 else [down, up]
    count = len(hops)

    chunk = 2 * TILE if tiles % 2 == 0 else TILE
    bf16, f32 = jnp.bfloat16, jnp.float32
    sums, gain, slot, q_all, k_all, *edges = pl.pallas_call(
        functools.partial(sums_kernel, chunk),
        out_shape=[
            pltpu.VMEM((2 * tiles, TILE), f32),
            pltpu.VMEM((2, width), f32),
            pltpu.VMEM((tiles * slots, TILE), jnp.int32),
            pltpu.VMEM((rows, width), bf16),
            pltpu.VMEM((rows, width), bf16),
        ]
        + [pltpu.VMEM((2, TILE, width), bf16)] * count,
        in_specs=[HBM] * 6,
        out_specs=[VMEM] * (5 + count),
        scratch_shapes=[
            pltpu.SMEM((slots, 1, tiles), jnp.int32),
            pltpu.VMEM((2, width), f32),
            pltpu.VMEM((2, width), f32),
            pltpu.SemaphoreType.DMA((2, rows // chunk)),
            pltpu.SemaphoreType.DMA((count, 2)),
            pltpu.SemaphoreType.DMA((3,)),
        ],
        compiler_params=pltpu.CompilerParams(vmem_limit_bytes=61 * MIB),
        cost_estimate=pl.CostEstimate(flops=4 * rows * width, bytes_accessed=4 * rows * width, transcendentals=0),
        name="sums",
    )(jnp.transpose(neighbours, (2, 0, 1)), q_gain, k_gain, q_rows, k_rows, v_rows)

    small = pltpu.CompilerParams(vmem_limit_bytes=1 * MIB)
    add = pl.pallas_call(
        add_kernel, out_shape=pltpu.VMEM((2 * tiles, TILE), f32), in_specs=[VMEM] * 2, out_specs=VMEM,
        compiler_params=small, name="add",
    )
    received = lax.ppermute(sums, "mp", [(i, i ^ 1) for i in range(groups)])
    edges = [lax.ppermute(edge, "seq", hop) for edge, hop in zip(edges, hops)]

    key_rows = rows + count * TILE
    early = (heads + 1) // 2
    step = timestep.reshape(1, 1)
    first = pl.pallas_call(
        first_kernel,
        out_shape=pltpu.VMEM((early, rows, key_rows), f32),
        in_specs=[VMEM] * 4,
        out_specs=VMEM,
        compiler_params=pltpu.CompilerParams(vmem_limit_bytes=8 * MIB),
        cost_estimate=pl.CostEstimate(flops=2 * rows * rows * early * DH, bytes_accessed=0, transcendentals=0),
        name="first",
    )(step, gain, q_all, k_all)
    received, first = lax.optimization_barrier((received, first))
    half = add(sums, received)
    received = lax.ppermute(half, "mp", [(i, i ^ 2) for i in range(groups)])
    first, second, v_all = pl.pallas_call(
        second_kernel,
        out_shape=[
            pltpu.VMEM((early, rows, key_rows), f32),
            pltpu.VMEM((heads - early, rows, key_rows), f32),
            pltpu.VMEM((key_rows, width), bf16),
        ],
        in_specs=[VMEM] * 5 + [HBM] + [VMEM] * (count + 1),
        out_specs=[VMEM] * 3,
        input_output_aliases={6 + count: 0},
        scratch_shapes=[pltpu.SemaphoreType.DMA((1 + count,))],
        compiler_params=pltpu.CompilerParams(vmem_limit_bytes=8 * MIB),
        cost_estimate=pl.CostEstimate(flops=2 * rows * rows * early * DH, bytes_accessed=0, transcendentals=0),
        name="second",
    )(half, step, gain, q_all, k_all, v_rows, *edges, first)
    received, first, second, v_all = lax.optimization_barrier((received, first, second, v_all))
    total, border = pl.pallas_call(
        total_kernel,
        out_shape=[pltpu.VMEM((2 * tiles, TILE), f32), pltpu.VMEM((2, TILE), f32)],
        in_specs=[VMEM] * 2, out_specs=[VMEM] * 2, compiler_params=small, name="total",
    )(half, received)
    borders = [lax.ppermute(border, "seq", hop) for hop in hops]

    def scaled(first_tile, borders, first, second):
        at = 1 + len(borders)
        return pl.pallas_call(
            functools.partial(scale_kernel, width * groups, first_tile),
            out_shape=[pltpu.VMEM(first.shape, f32), pltpu.VMEM(second.shape, f32)],
            in_specs=[VMEM] * (at + 2),
            out_specs=[VMEM] * 2,
            input_output_aliases={at: 0, at + 1: 1},
            compiler_params=small,
            cost_estimate=pl.CostEstimate(flops=rows * rows * heads, bytes_accessed=0, transcendentals=0),
            name="scale",
        )(total, *borders, first, second)

    first, second = scaled(0, [], first, second)
    borders, first, second = lax.optimization_barrier((borders, first, second))
    first, second = scaled(tiles, borders, first, second)

    pairs = tiles * slots * TILE * TILE * heads
    mixed = pl.pallas_call(
        functools.partial(attention_kernel, tiles),
        out_shape=jax.ShapeDtypeStruct((rows, width), bf16),
        in_specs=[VMEM] * 4,
        out_specs=HBM,
        scratch_shapes=[pltpu.VMEM((rows, width), bf16), pltpu.SemaphoreType.DMA((tiles,))],
        compiler_params=pltpu.CompilerParams(vmem_limit_bytes=24 * MIB),
        cost_estimate=pl.CostEstimate(flops=2 * pairs * DH, bytes_accessed=2 * rows * width, transcendentals=pairs),
        name="attention",
    )(slot, first, second, v_all)
    return mixed.reshape(1, rows, width)


def solution(mesh):
    return jax.shard_map(
        shards,
        mesh=mesh,
        in_specs=(
            P("expert", "seq", "mp"),
            P("expert", "seq", "mp"),
            P("expert", "seq", "mp"),
            P("expert"),
            P("expert", "seq", None),
            P(None, "mp"),
            P(None, "mp"),
        ),
        out_specs=P("expert", "seq", "mp"),
        check_vma=False,
    )
```

```python
import functools

import jax
import jax.numpy as jnp
from jax import lax
from jax.experimental import pallas as pl
from jax.experimental.pallas import tpu as pltpu
from jax.sharding import PartitionSpec as P

DH = 128
TILE = 128
EPSILON = 1e-06
SWITCH_STEP = 875
LOG2E = 1.4426950408889634
MIB = 1 << 20
DEPTH = 1

HBM = pl.BlockSpec(memory_space=pltpu.HBM)
VMEM = pl.BlockSpec(memory_space=pltpu.VMEM)
SMEM = pl.BlockSpec(memory_space=pltpu.SMEM)


def tile_rows(index):
    if isinstance(index, int):
        return pl.ds(index * TILE, TILE)
    return pl.ds(pl.multiple_of(index * TILE, TILE), TILE)


def sums_kernel(chunk, near_hbm, gq_hbm, gk_hbm, q_hbm, k_hbm, v_hbm, sums_ref, gain_ref, slot_ref,
                q_ref, k_ref, *rest):
    *edges, near, gq, gk, sems, edge_sems, small_sems = rest
    rows, width = q_hbm.shape
    tiles, slots = rows // TILE, near_hbm.shape[0]
    place = lax.axis_index("seq")
    copies = []
    for a, (src, dst) in enumerate(((q_hbm, q_ref), (k_hbm, k_ref))):
        for j in range(rows // chunk):
            part = pl.ds(j * chunk, chunk)
            copies.append(pltpu.make_async_copy(src.at[part], dst.at[part], sems.at[a, j]))
            copies[-1].start()
    small = [
        pltpu.make_async_copy(src, dst, small_sems.at[a])
        for a, (src, dst) in enumerate(((near_hbm, near), (gq_hbm, gq), (gk_hbm, gk)))
    ]
    for copy in small:
        copy.start()
    edge_copies = []
    for e, edge in enumerate(edges):
        first = jnp.where(place == 0, tiles - 1, 0) if len(edges) == 1 else (0, tiles - 1)[e]
        for a, src in enumerate((k_hbm, v_hbm)):
            edge_copies.append(pltpu.make_async_copy(src.at[tile_rows(first)], edge.at[a], edge_sems.at[e, a]))
            edge_copies[-1].start()
    diagonal = lax.broadcasted_iota(jnp.int32, (TILE, TILE), 0) == lax.broadcasted_iota(
        jnp.int32, (TILE, TILE), 1
    )
    for a, buf in enumerate((q_ref, k_ref)):
        for t in range(tiles):
            if t * TILE % chunk == 0:
                copies[a * (rows // chunk) + t * TILE // chunk].wait()
            total = 0.0
            for j in range(width // DH):
                x = buf[t * TILE : (t + 1) * TILE, j * DH : (j + 1) * DH].astype(jnp.float32)
                total = total + x * x
            total = jnp.sum(total, axis=1, keepdims=True)
            total = jnp.sum(jnp.where(diagonal, total, 0.0), axis=0, keepdims=True)
            sums_ref[a * tiles + t : a * tiles + t + 1, :] = total
        if a == 0:
            for copy in small:
                copy.wait()
            gain_ref[...] = gq[...] * gk[...] * (DH ** -0.5 * LOG2E)
            for i in range(tiles):
                for n in range(slots):
                    local = near[n, 0, i] - place * tiles
                    local = jnp.where(local < 0, tiles + len(edges) - 1, jnp.minimum(local, tiles))
                    slot_ref[i * slots + n] = local
    for copy in edge_copies:
        copy.wait()


def add_kernel(a_ref, b_ref, out_ref):
    out_ref[...] = a_ref[...] + b_ref[...]


def total_kernel(a_ref, b_ref, out_ref, border_ref):
    total = a_ref[...] + b_ref[...]
    out_ref[...] = total
    tiles = total.shape[0] // 2
    border_ref[0:1, :] = total[tiles : tiles + 1]
    border_ref[1:2, :] = total[2 * tiles - 1 : 2 * tiles]


def expert_gain(step_ref, gain_ref):
    return jnp.where(step_ref[...] >= SWITCH_STEP, gain_ref[0:1, :], gain_ref[1:2, :])


def own_scores(gain, q_ref, k_ref, score_ref, at, h):
    cols = slice(h * DH, (h + 1) * DH)
    query = (q_ref[:, cols].astype(jnp.float32) * gain[:, cols]).astype(jnp.bfloat16)
    rows = k_ref.shape[0]
    for j in range(0, rows, 2 * TILE):
        end = min(j + 2 * TILE, rows)
        score_ref[at, :, j:end] = lax.dot_general(
            query, k_ref[j:end, cols], (((1,), (1,)), ((), ())), preferred_element_type=jnp.float32
        )


def first_kernel(step_ref, gain_ref, q_ref, k_ref, score_ref):
    gain = expert_gain(step_ref, gain_ref)
    for h in range(score_ref.shape[0]):
        own_scores(gain, q_ref, k_ref, score_ref, h, h)


def second_kernel(half_ref, step_ref, gain_ref, q_ref, k_ref, v_hbm, *rest):
    del half_ref
    *edges, given_ref, first_ref, score_ref, v_ref, sems = rest
    del given_ref
    rows = q_ref.shape[0]
    copies = [pltpu.make_async_copy(v_hbm, v_ref.at[pl.ds(0, rows)], sems.at[0])]
    for e, edge in enumerate(edges):
        part = pl.ds(rows + e * TILE, TILE)
        copies.append(pltpu.make_async_copy(edge.at[1], v_ref.at[part], sems.at[1 + e]))
    for copy in copies:
        copy.start()
    gain = expert_gain(step_ref, gain_ref)
    done = first_ref.shape[0]
    for h in range(done + score_ref.shape[0]):
        cols = slice(h * DH, (h + 1) * DH)
        out_ref, at = (first_ref, h) if h < done else (score_ref, h - done)
        if h >= done:
            own_scores(gain, q_ref, k_ref, score_ref, at, h)
        query = (q_ref[:, cols].astype(jnp.float32) * gain[:, cols]).astype(jnp.bfloat16)
        for e, edge in enumerate(edges):
            out_ref[at, :, rows + e * TILE : rows + (e + 1) * TILE] = lax.dot_general(
                query, edge[0, :, cols], (((1,), (1,)), ((), ())), preferred_element_type=jnp.float32
            )
    for copy in copies:
        copy.wait()


def scale_kernel(full_width, first_tile, sums_ref, *rest):
    *borders, _, _, first_ref, second_ref = rest
    tiles = sums_ref.shape[0] // 2

    def scale(sums):
        return lax.rsqrt(sums * (1.0 / full_width) + EPSILON)

    if not borders:
        k_scale = [scale(sums_ref[tiles + t : tiles + t + 1, :]) for t in range(tiles)]
    elif len(borders) == 1:
        place = lax.axis_index("seq")
        k_scale = [scale(jnp.where(place == 0, borders[0][0:1, :], borders[0][1:2, :]))]
    else:
        k_scale = [scale(borders[0][0:1, :]), scale(borders[1][1:2, :])]
    q_scale = scale(sums_ref[0:tiles, :])
    q_scale = jnp.concatenate([q_scale, jnp.zeros((8 - tiles % 8, TILE), jnp.float32)], axis=0).T
    for i in range(tiles):
        column = jnp.broadcast_to(q_scale[:, i : i + 1], (TILE, TILE))
        rows = slice(i * TILE, (i + 1) * TILE)
        for t, row in enumerate(k_scale):
            both = column * row
            cols = slice((first_tile + t) * TILE, (first_tile + t + 1) * TILE)
            for ref in (first_ref, second_ref):
                for h in range(ref.shape[0]):
                    ref[h, rows, cols] = ref[h, rows, cols] * both


def attention_kernel(tiles, slot_ref, first_ref, second_ref, v_ref, out_hbm, out_buf, sems):
    slots = slot_ref.shape[0] // tiles
    done = first_ref.shape[0]
    heads = done + second_ref.shape[0]
    slot = [[slot_ref[i * slots + n] for n in range(slots)] for i in range(tiles)]
    ones = jnp.ones((TILE, DH), jnp.bfloat16)

    def weights(i, h):
        score_ref, at = (first_ref, h) if h < done else (second_ref, h - done)
        rows = pl.ds(i * TILE, TILE)
        score = [score_ref[at, rows, tile_rows(slot[i][n])] for n in range(slots)]
        top = jnp.max(functools.reduce(jnp.maximum, score), axis=1, keepdims=True)
        return jnp.concatenate([jnp.exp2(x - top).astype(jnp.bfloat16) for x in score], axis=1)

    def mix(i, h, weight):
        cols = slice(h * DH, (h + 1) * DH)
        value = jnp.concatenate(
            [jnp.concatenate([v_ref[tile_rows(slot[i][n]), cols], ones], axis=1) for n in range(slots)],
            axis=0,
        )
        return jnp.dot(weight, value, preferred_element_type=jnp.float32)

    def finish(i, h, mixed):
        rows = pl.ds(i * TILE, TILE)
        out_buf[rows, h * DH : (h + 1) * DH] = (mixed[:, :DH] / mixed[:, DH:]).astype(jnp.bfloat16)
        if h == heads - 1:
            pltpu.make_async_copy(out_buf.at[rows], out_hbm.at[rows], sems.at[i]).start()

    pairs = [(i, h) for i in range(tiles) for h in range(heads)]
    weight, mixed = {}, {}
    for s in range(len(pairs) + DEPTH + 1):
        if s < len(pairs):
            weight[s] = weights(*pairs[s])
        if DEPTH <= s < len(pairs) + DEPTH:
            mixed[s - DEPTH] = mix(*pairs[s - DEPTH], weight.pop(s - DEPTH))
        if s > DEPTH:
            finish(*pairs[s - DEPTH - 1], mixed.pop(s - DEPTH - 1))
    for i in range(tiles):
        rows = pl.ds(i * TILE, TILE)
        pltpu.make_async_copy(out_buf.at[rows], out_hbm.at[rows], sems.at[i]).wait()


def shards(queries, key_input, value_input, timestep, neighbours, q_gain, k_gain):
    q_rows, k_rows, v_rows = queries[0], key_input[0], value_input[0]
    rows, width = q_rows.shape
    tiles, heads = rows // TILE, width // DH
    slots = neighbours.shape[2]
    groups, devices = lax.axis_size("mp"), lax.axis_size("seq")

    up = [(i, (i + 1) % devices) for i in range(devices)]
    down = [(i, (i - 1) % devices) for i in range(devices)]
    hops = [up] if devices == 2 else [down, up]
    count = len(hops)

    chunk = 2 * TILE if tiles % 2 == 0 else TILE
    bf16, f32 = jnp.bfloat16, jnp.float32
    sums, gain, slot, q_all, k_all, *edges = pl.pallas_call(
        functools.partial(sums_kernel, chunk),
        out_shape=[
            pltpu.VMEM((2 * tiles, TILE), f32),
            pltpu.VMEM((2, width), f32),
            pltpu.SMEM((tiles * slots,), jnp.int32),
            pltpu.VMEM((rows, width), bf16),
            pltpu.VMEM((rows, width), bf16),
        ]
        + [pltpu.VMEM((2, TILE, width), bf16)] * count,
        in_specs=[HBM] * 6,
        out_specs=[VMEM, VMEM, SMEM] + [VMEM] * (2 + count),
        scratch_shapes=[
            pltpu.SMEM((slots, 1, tiles), jnp.int32),
            pltpu.VMEM((2, width), f32),
            pltpu.VMEM((2, width), f32),
            pltpu.SemaphoreType.DMA((2, rows // chunk)),
            pltpu.SemaphoreType.DMA((count, 2)),
            pltpu.SemaphoreType.DMA((3,)),
        ],
        compiler_params=pltpu.CompilerParams(vmem_limit_bytes=61 * MIB),
        cost_estimate=pl.CostEstimate(flops=4 * rows * width, bytes_accessed=4 * rows * width, transcendentals=0),
        name="sums",
    )(jnp.transpose(neighbours, (2, 0, 1)), q_gain, k_gain, q_rows, k_rows, v_rows)

    small = pltpu.CompilerParams(vmem_limit_bytes=1 * MIB)
    add = pl.pallas_call(
        add_kernel, out_shape=pltpu.VMEM((2 * tiles, TILE), f32), in_specs=[VMEM] * 2, out_specs=VMEM,
        compiler_params=small, name="add",
    )
    received = lax.ppermute(sums, "mp", [(i, i ^ 1) for i in range(groups)])
    edges = [lax.ppermute(edge, "seq", hop) for edge, hop in zip(edges, hops)]

    key_rows = rows + count * TILE
    early = (heads + 1) // 2
    step = timestep.reshape(1, 1)
    first = pl.pallas_call(
        first_kernel,
        out_shape=pltpu.VMEM((early, rows, key_rows), f32),
        in_specs=[VMEM] * 4,
        out_specs=VMEM,
        compiler_params=pltpu.CompilerParams(vmem_limit_bytes=8 * MIB),
        cost_estimate=pl.CostEstimate(flops=2 * rows * rows * early * DH, bytes_accessed=0, transcendentals=0),
        name="first",
    )(step, gain, q_all, k_all)
    received, first = lax.optimization_barrier((received, first))
    half = add(sums, received)
    received = lax.ppermute(half, "mp", [(i, i ^ 2) for i in range(groups)])
    first, second, v_all = pl.pallas_call(
        second_kernel,
        out_shape=[
            pltpu.VMEM((early, rows, key_rows), f32),
            pltpu.VMEM((heads - early, rows, key_rows), f32),
            pltpu.VMEM((key_rows, width), bf16),
        ],
        in_specs=[VMEM] * 5 + [HBM] + [VMEM] * (count + 1),
        out_specs=[VMEM] * 3,
        input_output_aliases={6 + count: 0},
        scratch_shapes=[pltpu.SemaphoreType.DMA((1 + count,))],
        compiler_params=pltpu.CompilerParams(vmem_limit_bytes=8 * MIB),
        cost_estimate=pl.CostEstimate(flops=2 * rows * rows * early * DH, bytes_accessed=0, transcendentals=0),
        name="second",
    )(half, step, gain, q_all, k_all, v_rows, *edges, first)
    received, first, second, v_all = lax.optimization_barrier((received, first, second, v_all))
    total, border = pl.pallas_call(
        total_kernel,
        out_shape=[pltpu.VMEM((2 * tiles, TILE), f32), pltpu.VMEM((2, TILE), f32)],
        in_specs=[VMEM] * 2, out_specs=[VMEM] * 2, compiler_params=small, name="total",
    )(half, received)
    borders = [lax.ppermute(border, "seq", hop) for hop in hops]

    def scaled(first_tile, borders, first, second):
        at = 1 + len(borders)
        return pl.pallas_call(
            functools.partial(scale_kernel, width * groups, first_tile),
            out_shape=[pltpu.VMEM(first.shape, f32), pltpu.VMEM(second.shape, f32)],
            in_specs=[VMEM] * (at + 2),
            out_specs=[VMEM] * 2,
            input_output_aliases={at: 0, at + 1: 1},
            compiler_params=small,
            cost_estimate=pl.CostEstimate(flops=rows * rows * heads, bytes_accessed=0, transcendentals=0),
            name="scale",
        )(total, *borders, first, second)

    first, second = scaled(0, [], first, second)
    borders, first, second = lax.optimization_barrier((borders, first, second))
    first, second = scaled(tiles, borders, first, second)

    pairs = tiles * slots * TILE * TILE * heads
    mixed = pl.pallas_call(
        functools.partial(attention_kernel, tiles),
        out_shape=jax.ShapeDtypeStruct((rows, width), bf16),
        in_specs=[SMEM] + [VMEM] * 3,
        out_specs=HBM,
        scratch_shapes=[pltpu.VMEM((rows, width), bf16), pltpu.SemaphoreType.DMA((tiles,))],
        compiler_params=pltpu.CompilerParams(vmem_limit_bytes=24 * MIB),
        cost_estimate=pl.CostEstimate(flops=2 * pairs * DH, bytes_accessed=2 * rows * width, transcendentals=pairs),
        name="attention",
    )(slot, first, second, v_all)
    return mixed.reshape(1, rows, width)


def solution(mesh):
    return jax.shard_map(
        shards,
        mesh=mesh,
        in_specs=(
            P("expert", "seq", "mp"),
            P("expert", "seq", "mp"),
            P("expert", "seq", "mp"),
            P("expert"),
            P("expert", "seq", None),
            P(None, "mp"),
            P(None, "mp"),
        ),
        out_specs=P("expert", "seq", "mp"),
        check_vma=False,
    )
```

```python
import functools

import jax
import jax.numpy as jnp
from jax import lax
from jax.experimental import pallas as pl
from jax.experimental.pallas import tpu as pltpu
from jax.sharding import PartitionSpec as P

DH = 128
TILE = 128
EPSILON = 1e-06
SWITCH_STEP = 875
LOG2E = 1.4426950408889634
MIB = 1 << 20
DEPTH = 1

HBM = pl.BlockSpec(memory_space=pltpu.HBM)
VMEM = pl.BlockSpec(memory_space=pltpu.VMEM)
SMEM = pl.BlockSpec(memory_space=pltpu.SMEM)


def tile_rows(index):
    if isinstance(index, int):
        return pl.ds(index * TILE, TILE)
    return pl.ds(pl.multiple_of(index * TILE, TILE), TILE)


def sums_kernel(chunk, near_hbm, gq_hbm, gk_hbm, q_hbm, k_hbm, v_hbm, sums_ref, gain_ref, slot_ref,
                q_ref, k_ref, *rest):
    *edges, near, gq, gk, sems, edge_sems, small_sems = rest
    rows, width = q_hbm.shape
    tiles, slots = rows // TILE, near_hbm.shape[0]
    place = lax.axis_index("seq")
    copies = []
    for a, (src, dst) in enumerate(((q_hbm, q_ref), (k_hbm, k_ref))):
        for j in range(rows // chunk):
            part = pl.ds(j * chunk, chunk)
            copies.append(pltpu.make_async_copy(src.at[part], dst.at[part], sems.at[a, j]))
            copies[-1].start()
    small = [
        pltpu.make_async_copy(src, dst, small_sems.at[a])
        for a, (src, dst) in enumerate(((near_hbm, near), (gq_hbm, gq), (gk_hbm, gk)))
    ]
    for copy in small:
        copy.start()
    edge_copies = []
    for e, edge in enumerate(edges):
        first = jnp.where(place == 0, tiles - 1, 0) if len(edges) == 1 else (0, tiles - 1)[e]
        for a, src in enumerate((k_hbm, v_hbm)):
            edge_copies.append(pltpu.make_async_copy(src.at[tile_rows(first)], edge.at[a], edge_sems.at[e, a]))
            edge_copies[-1].start()
    diagonal = lax.broadcasted_iota(jnp.int32, (TILE, TILE), 0) == lax.broadcasted_iota(
        jnp.int32, (TILE, TILE), 1
    )
    for a, buf in enumerate((q_ref, k_ref)):
        for t in range(tiles):
            if t * TILE % chunk == 0:
                copies[a * (rows // chunk) + t * TILE // chunk].wait()
            total = 0.0
            for j in range(width // DH):
                x = buf[t * TILE : (t + 1) * TILE, j * DH : (j + 1) * DH].astype(jnp.float32)
                total = total + x * x
            total = jnp.sum(total, axis=1, keepdims=True)
            total = jnp.sum(jnp.where(diagonal, total, 0.0), axis=0, keepdims=True)
            sums_ref[a * tiles + t : a * tiles + t + 1, :] = total
        if a == 0:
            for copy in small:
                copy.wait()
            gain_ref[...] = gq[...] * gk[...] * (DH ** -0.5 * LOG2E)
            for i in range(tiles):
                for n in range(slots):
                    local = near[n, 0, i] - place * tiles
                    local = jnp.where(local < 0, tiles + len(edges) - 1, jnp.minimum(local, tiles))
                    slot_ref[i * slots + n] = local
    for copy in edge_copies:
        copy.wait()


def add_kernel(a_ref, b_ref, out_ref):
    out_ref[...] = a_ref[...] + b_ref[...]


def total_kernel(a_ref, b_ref, out_ref, border_ref):
    total = a_ref[...] + b_ref[...]
    out_ref[...] = total
    tiles = total.shape[0] // 2
    border_ref[0:1, :] = total[tiles : tiles + 1]
    border_ref[1:2, :] = total[2 * tiles - 1 : 2 * tiles]


def expert_gain(step_ref, gain_ref):
    return jnp.where(step_ref[...] >= SWITCH_STEP, gain_ref[0:1, :], gain_ref[1:2, :])


def own_scores(gain, q_ref, k_ref, score_ref, at, h):
    cols = slice(h * DH, (h + 1) * DH)
    query = (q_ref[:, cols].astype(jnp.float32) * gain[:, cols]).astype(jnp.bfloat16)
    rows = k_ref.shape[0]
    for j in range(0, rows, 2 * TILE):
        end = min(j + 2 * TILE, rows)
        score = lax.dot_general(
            query, k_ref[j:end, cols], (((1,), (1,)), ((), ())), preferred_element_type=jnp.float32
        )
        for c in range(0, end - j, TILE):
            score_ref[at, (j + c) // TILE] = score[:, c : c + TILE]


def first_kernel(step_ref, gain_ref, q_ref, k_ref, score_ref):
    gain = expert_gain(step_ref, gain_ref)
    for h in range(score_ref.shape[0]):
        own_scores(gain, q_ref, k_ref, score_ref, h, h)


def second_kernel(half_ref, step_ref, gain_ref, q_ref, k_ref, v_hbm, *rest):
    del half_ref
    *edges, given_ref, first_ref, score_ref, v_ref, sems = rest
    del given_ref
    rows = q_ref.shape[0]
    copies = [pltpu.make_async_copy(v_hbm, v_ref.at[pl.ds(0, rows)], sems.at[0])]
    for e, edge in enumerate(edges):
        part = pl.ds(rows + e * TILE, TILE)
        copies.append(pltpu.make_async_copy(edge.at[1], v_ref.at[part], sems.at[1 + e]))
    for copy in copies:
        copy.start()
    gain = expert_gain(step_ref, gain_ref)
    done = first_ref.shape[0]
    for h in range(done + score_ref.shape[0]):
        cols = slice(h * DH, (h + 1) * DH)
        out_ref, at = (first_ref, h) if h < done else (score_ref, h - done)
        if h >= done:
            own_scores(gain, q_ref, k_ref, score_ref, at, h)
        query = (q_ref[:, cols].astype(jnp.float32) * gain[:, cols]).astype(jnp.bfloat16)
        for e, edge in enumerate(edges):
            out_ref[at, rows // TILE + e] = lax.dot_general(
                query, edge[0, :, cols], (((1,), (1,)), ((), ())), preferred_element_type=jnp.float32
            )
    for copy in copies:
        copy.wait()


def scale_kernel(full_width, sums_ref, *rest):
    *borders, _, _, first_ref, second_ref = rest
    tiles = sums_ref.shape[0] // 2

    def scale(sums):
        return lax.rsqrt(sums * (1.0 / full_width) + EPSILON)

    refs = (first_ref, second_ref)
    if borders:
        if len(borders) == 1:
            place = lax.axis_index("seq")
            k_scale = [scale(jnp.where(place == 0, borders[0][0:1, :], borders[0][1:2, :]))]
        else:
            k_scale = [scale(borders[0][0:1, :]), scale(borders[1][1:2, :])]
        for t, row in enumerate(k_scale):
            for ref in refs:
                for h in range(ref.shape[0]):
                    ref[h, tiles + t] = ref[h, tiles + t] * row
    else:
        k_scale = [scale(sums_ref[tiles + t : tiles + t + 1, :]) for t in range(tiles)]
        q_scale = scale(sums_ref[0:tiles, :])
        q_scale = jnp.concatenate([q_scale, jnp.zeros((8 - tiles % 8, TILE), jnp.float32)], axis=0).T
        for i in range(tiles):
            column = jnp.broadcast_to(q_scale[:, i : i + 1], (TILE, TILE))
            rows = slice(i * TILE, (i + 1) * TILE)
            for t in range(first_ref.shape[1]):
                both = column * k_scale[t] if t < tiles else column
                for ref in refs:
                    for h in range(ref.shape[0]):
                        ref[h, t, rows, :] = ref[h, t, rows, :] * both


def attention_kernel(tiles, slot_ref, first_ref, second_ref, v_ref, out_hbm, out_buf, sems):
    slots = slot_ref.shape[0] // tiles
    done = first_ref.shape[0]
    heads = done + second_ref.shape[0]
    slot = [[slot_ref[i * slots + n] for n in range(slots)] for i in range(tiles)]
    ones = jnp.ones((TILE, DH), jnp.bfloat16)

    def weights(i, h):
        score_ref, at = (first_ref, h) if h < done else (second_ref, h - done)
        rows = pl.ds(i * TILE, TILE)
        score = [score_ref[at, slot[i][n], rows, :] for n in range(slots)]
        top = jnp.max(functools.reduce(jnp.maximum, score), axis=1, keepdims=True)
        return jnp.concatenate([jnp.exp2(x - top).astype(jnp.bfloat16) for x in score], axis=1)

    def mix(i, h, weight):
        cols = slice(h * DH, (h + 1) * DH)
        value = jnp.concatenate(
            [jnp.concatenate([v_ref[tile_rows(slot[i][n]), cols], ones], axis=1) for n in range(slots)],
            axis=0,
        )
        return jnp.dot(weight, value, preferred_element_type=jnp.float32)

    def finish(i, h, mixed):
        rows = pl.ds(i * TILE, TILE)
        out_buf[rows, h * DH : (h + 1) * DH] = (mixed[:, :DH] / mixed[:, DH:]).astype(jnp.bfloat16)
        if h == heads - 1:
            pltpu.make_async_copy(out_buf.at[rows], out_hbm.at[rows], sems.at[i]).start()

    pairs = [(i, h) for i in range(tiles) for h in range(heads)]
    weight, mixed = {}, {}
    for s in range(len(pairs) + DEPTH + 1):
        if s < len(pairs):
            weight[s] = weights(*pairs[s])
        if DEPTH <= s < len(pairs) + DEPTH:
            mixed[s - DEPTH] = mix(*pairs[s - DEPTH], weight.pop(s - DEPTH))
        if s > DEPTH:
            finish(*pairs[s - DEPTH - 1], mixed.pop(s - DEPTH - 1))
    for i in range(tiles):
        rows = pl.ds(i * TILE, TILE)
        pltpu.make_async_copy(out_buf.at[rows], out_hbm.at[rows], sems.at[i]).wait()


def shards(queries, key_input, value_input, timestep, neighbours, q_gain, k_gain):
    q_rows, k_rows, v_rows = queries[0], key_input[0], value_input[0]
    rows, width = q_rows.shape
    tiles, heads = rows // TILE, width // DH
    slots = neighbours.shape[2]
    groups, devices = lax.axis_size("mp"), lax.axis_size("seq")

    up = [(i, (i + 1) % devices) for i in range(devices)]
    down = [(i, (i - 1) % devices) for i in range(devices)]
    hops = [up] if devices == 2 else [down, up]
    count = len(hops)

    chunk = rows // 2 if tiles % 2 == 0 else TILE
    bf16, f32 = jnp.bfloat16, jnp.float32
    sums, gain, slot, q_all, k_all, *edges = pl.pallas_call(
        functools.partial(sums_kernel, chunk),
        out_shape=[
            pltpu.VMEM((2 * tiles, TILE), f32),
            pltpu.VMEM((2, width), f32),
            pltpu.SMEM((tiles * slots,), jnp.int32),
            pltpu.VMEM((rows, width), bf16),
            pltpu.VMEM((rows, width), bf16),
        ]
        + [pltpu.VMEM((2, TILE, width), bf16)] * count,
        in_specs=[HBM] * 6,
        out_specs=[VMEM, VMEM, SMEM] + [VMEM] * (2 + count),
        scratch_shapes=[
            pltpu.SMEM((slots, 1, tiles), jnp.int32),
            pltpu.VMEM((2, width), f32),
            pltpu.VMEM((2, width), f32),
            pltpu.SemaphoreType.DMA((2, rows // chunk)),
            pltpu.SemaphoreType.DMA((count, 2)),
            pltpu.SemaphoreType.DMA((3,)),
        ],
        compiler_params=pltpu.CompilerParams(vmem_limit_bytes=61 * MIB),
        cost_estimate=pl.CostEstimate(flops=4 * rows * width, bytes_accessed=4 * rows * width, transcendentals=0),
        name="sums",
    )(jnp.transpose(neighbours, (2, 0, 1)), q_gain, k_gain, q_rows, k_rows, v_rows)

    small = pltpu.CompilerParams(vmem_limit_bytes=1 * MIB)
    add = pl.pallas_call(
        add_kernel, out_shape=pltpu.VMEM((2 * tiles, TILE), f32), in_specs=[VMEM] * 2, out_specs=VMEM,
        compiler_params=small, name="add",
    )
    received = lax.ppermute(sums, "mp", [(i, i ^ 1) for i in range(groups)])
    edges = [lax.ppermute(edge, "seq", hop) for edge, hop in zip(edges, hops)]

    key_rows = rows + count * TILE
    early = (heads + 1) // 2
    step = timestep.reshape(1, 1)
    first = pl.pallas_call(
        first_kernel,
        out_shape=pltpu.VMEM((early, key_rows // TILE, rows, TILE), f32),
        in_specs=[VMEM] * 4,
        out_specs=VMEM,
        compiler_params=pltpu.CompilerParams(vmem_limit_bytes=8 * MIB),
        cost_estimate=pl.CostEstimate(flops=2 * rows * rows * early * DH, bytes_accessed=0, transcendentals=0),
        name="first",
    )(step, gain, q_all, k_all)
    received, first = lax.optimization_barrier((received, first))
    half = add(sums, received)
    received = lax.ppermute(half, "mp", [(i, i ^ 2) for i in range(groups)])
    first, second, v_all = pl.pallas_call(
        second_kernel,
        out_shape=[
            pltpu.VMEM((early, key_rows // TILE, rows, TILE), f32),
            pltpu.VMEM((heads - early, key_rows // TILE, rows, TILE), f32),
            pltpu.VMEM((key_rows, width), bf16),
        ],
        in_specs=[VMEM] * 5 + [HBM] + [VMEM] * (count + 1),
        out_specs=[VMEM] * 3,
        input_output_aliases={6 + count: 0},
        scratch_shapes=[pltpu.SemaphoreType.DMA((1 + count,))],
        compiler_params=pltpu.CompilerParams(vmem_limit_bytes=8 * MIB),
        cost_estimate=pl.CostEstimate(flops=2 * rows * rows * early * DH, bytes_accessed=0, transcendentals=0),
        name="second",
    )(half, step, gain, q_all, k_all, v_rows, *edges, first)
    received, first, second, v_all = lax.optimization_barrier((received, first, second, v_all))
    total, border = pl.pallas_call(
        total_kernel,
        out_shape=[pltpu.VMEM((2 * tiles, TILE), f32), pltpu.VMEM((2, TILE), f32)],
        in_specs=[VMEM] * 2, out_specs=[VMEM] * 2, compiler_params=small, name="total",
    )(half, received)
    borders = [lax.ppermute(border, "seq", hop) for hop in hops]

    def scaled(borders, first, second):
        at = 1 + len(borders)
        return pl.pallas_call(
            functools.partial(scale_kernel, width * groups),
            out_shape=[pltpu.VMEM(first.shape, f32), pltpu.VMEM(second.shape, f32)],
            in_specs=[VMEM] * (at + 2),
            out_specs=[VMEM] * 2,
            input_output_aliases={at: 0, at + 1: 1},
            compiler_params=small,
            cost_estimate=pl.CostEstimate(flops=rows * rows * heads, bytes_accessed=0, transcendentals=0),
            name="scale",
        )(total, *borders, first, second)

    first, second = scaled([], first, second)
    borders, first, second = lax.optimization_barrier((borders, first, second))
    first, second = scaled(borders, first, second)

    pairs = tiles * slots * TILE * TILE * heads
    mixed = pl.pallas_call(
        functools.partial(attention_kernel, tiles),
        out_shape=jax.ShapeDtypeStruct((rows, width), bf16),
        in_specs=[SMEM] + [VMEM] * 3,
        out_specs=HBM,
        scratch_shapes=[pltpu.VMEM((rows, width), bf16), pltpu.SemaphoreType.DMA((tiles,))],
        compiler_params=pltpu.CompilerParams(vmem_limit_bytes=24 * MIB),
        cost_estimate=pl.CostEstimate(flops=2 * pairs * DH, bytes_accessed=2 * rows * width, transcendentals=pairs),
        name="attention",
    )(slot, first, second, v_all)
    return mixed.reshape(1, rows, width)


def solution(mesh):
    return jax.shard_map(
        shards,
        mesh=mesh,
        in_specs=(
            P("expert", "seq", "mp"),
            P("expert", "seq", "mp"),
            P("expert", "seq", "mp"),
            P("expert"),
            P("expert", "seq", None),
            P(None, "mp"),
            P(None, "mp"),
        ),
        out_specs=P("expert", "seq", "mp"),
        check_vma=False,
    )
```

```python
import functools

import jax
import jax.numpy as jnp
from jax import lax
from jax.experimental import pallas as pl
from jax.experimental.pallas import tpu as pltpu
from jax.sharding import PartitionSpec as P

DH = 128
TILE = 128
EPSILON = 1e-06
SWITCH_STEP = 875
LOG2E = 1.4426950408889634
MIB = 1 << 20
DEPTH = 1

HBM = pl.BlockSpec(memory_space=pltpu.HBM)
VMEM = pl.BlockSpec(memory_space=pltpu.VMEM)
SMEM = pl.BlockSpec(memory_space=pltpu.SMEM)


def tile_rows(index):
    if isinstance(index, int):
        return pl.ds(index * TILE, TILE)
    return pl.ds(pl.multiple_of(index * TILE, TILE), TILE)


def sums_kernel(chunk, near_hbm, gq_hbm, gk_hbm, q_hbm, k_hbm, v_hbm, sums_ref, gain_ref, slot_ref,
                q_ref, k_ref, *rest):
    *edges, near, gq, gk, sems, edge_sems, small_sems = rest
    rows, width = q_hbm.shape
    tiles, slots = rows // TILE, near_hbm.shape[0]
    place = lax.axis_index("seq")
    copies = []
    for a, (src, dst) in enumerate(((q_hbm, q_ref), (k_hbm, k_ref))):
        for j in range(rows // chunk):
            part = pl.ds(j * chunk, chunk)
            copies.append(pltpu.make_async_copy(src.at[part], dst.at[part], sems.at[a, j]))
            copies[-1].start()
    small = [
        pltpu.make_async_copy(src, dst, small_sems.at[a])
        for a, (src, dst) in enumerate(((near_hbm, near), (gq_hbm, gq), (gk_hbm, gk)))
    ]
    for copy in small:
        copy.start()
    edge_copies = []
    for e, edge in enumerate(edges):
        first = jnp.where(place == 0, tiles - 1, 0) if len(edges) == 1 else (0, tiles - 1)[e]
        for a, src in enumerate((k_hbm, v_hbm)):
            edge_copies.append(pltpu.make_async_copy(src.at[tile_rows(first)], edge.at[a], edge_sems.at[e, a]))
            edge_copies[-1].start()
    diagonal = lax.broadcasted_iota(jnp.int32, (TILE, TILE), 0) == lax.broadcasted_iota(
        jnp.int32, (TILE, TILE), 1
    )
    for a, buf in enumerate((q_ref, k_ref)):
        for t in range(tiles):
            if t * TILE % chunk == 0:
                copies[a * (rows // chunk) + t * TILE // chunk].wait()
            total = 0.0
            for j in range(width // DH):
                x = buf[t * TILE : (t + 1) * TILE, j * DH : (j + 1) * DH].astype(jnp.float32)
                total = total + x * x
            total = jnp.sum(total, axis=1, keepdims=True)
            total = jnp.sum(jnp.where(diagonal, total, 0.0), axis=0, keepdims=True)
            sums_ref[a * tiles + t : a * tiles + t + 1, :] = total
        if a == 0:
            for copy in small:
                copy.wait()
            gain_ref[...] = gq[...] * gk[...] * (DH ** -0.5 * LOG2E)
            for i in range(tiles):
                for n in range(slots):
                    local = near[n, 0, i] - place * tiles
                    local = jnp.where(local < 0, tiles + len(edges) - 1, jnp.minimum(local, tiles))
                    slot_ref[i * slots + n] = local
    for copy in edge_copies:
        copy.wait()


def add_kernel(a_ref, b_ref, out_ref):
    out_ref[...] = a_ref[...] + b_ref[...]


def total_kernel(a_ref, b_ref, out_ref, border_ref):
    total = a_ref[...] + b_ref[...]
    out_ref[...] = total
    tiles = total.shape[0] // 2
    border_ref[0:1, :] = total[tiles : tiles + 1]
    border_ref[1:2, :] = total[2 * tiles - 1 : 2 * tiles]


def expert_gain(step_ref, gain_ref):
    return jnp.where(step_ref[...] >= SWITCH_STEP, gain_ref[0:1, :], gain_ref[1:2, :])


def own_scores(gain, q_ref, k_ref, score_ref, at, h):
    cols = slice(h * DH, (h + 1) * DH)
    query = (q_ref[:, cols].astype(jnp.float32) * gain[:, cols]).astype(jnp.bfloat16)
    rows = k_ref.shape[0]
    for j in range(0, rows, 2 * TILE):
        end = min(j + 2 * TILE, rows)
        score = lax.dot_general(
            query, k_ref[j:end, cols], (((1,), (1,)), ((), ())), preferred_element_type=jnp.float32
        )
        for c in range(0, end - j, TILE):
            score_ref[at, (j + c) // TILE] = score[:, c : c + TILE]


def first_kernel(step_ref, gain_ref, q_ref, k_ref, score_ref):
    gain = expert_gain(step_ref, gain_ref)
    for h in range(score_ref.shape[0]):
        own_scores(gain, q_ref, k_ref, score_ref, h, h)


def second_kernel(half_ref, step_ref, gain_ref, q_ref, k_ref, v_hbm, *rest):
    del half_ref
    *edges, given_ref, first_ref, score_ref, v_ref, sems = rest
    del given_ref
    rows = q_ref.shape[0]
    copies = [pltpu.make_async_copy(v_hbm, v_ref.at[pl.ds(0, rows)], sems.at[0])]
    for e, edge in enumerate(edges):
        part = pl.ds(rows + e * TILE, TILE)
        copies.append(pltpu.make_async_copy(edge.at[1], v_ref.at[part], sems.at[1 + e]))
    for copy in copies:
        copy.start()
    gain = expert_gain(step_ref, gain_ref)
    done = first_ref.shape[0]
    for h in range(done + score_ref.shape[0]):
        cols = slice(h * DH, (h + 1) * DH)
        out_ref, at = (first_ref, h) if h < done else (score_ref, h - done)
        if h >= done:
            own_scores(gain, q_ref, k_ref, score_ref, at, h)
        query = (q_ref[:, cols].astype(jnp.float32) * gain[:, cols]).astype(jnp.bfloat16)
        for e, edge in enumerate(edges):
            out_ref[at, rows // TILE + e] = lax.dot_general(
                query, edge[0, :, cols], (((1,), (1,)), ((), ())), preferred_element_type=jnp.float32
            )
    for copy in copies:
        copy.wait()


def scale_kernel(full_width, sums_ref, *rest):
    *borders, _, _, first_ref, second_ref, column_buf = rest
    tiles = sums_ref.shape[0] // 2

    def scale(sums):
        return lax.rsqrt(sums * (1.0 / full_width) + EPSILON)

    refs = (first_ref, second_ref)
    if borders:
        if len(borders) == 1:
            place = lax.axis_index("seq")
            k_scale = [scale(jnp.where(place == 0, borders[0][0:1, :], borders[0][1:2, :]))]
        else:
            k_scale = [scale(borders[0][0:1, :]), scale(borders[1][1:2, :])]
        for t, row in enumerate(k_scale):
            for ref in refs:
                for h in range(ref.shape[0]):
                    ref[h, tiles + t] = ref[h, tiles + t] * row
    else:
        k_scale = [scale(sums_ref[tiles + t : tiles + t + 1, :]) for t in range(tiles)]
        q_scale = scale(sums_ref[0:tiles, :])
        q_scale = jnp.concatenate([q_scale, jnp.zeros((8 - tiles % 8, TILE), jnp.float32)], axis=0).T
        k_scale += [jnp.ones((1, TILE), jnp.float32)] * (first_ref.shape[1] - tiles)
        for i in range(tiles):
            column_buf[i * TILE : (i + 1) * TILE, :] = jnp.broadcast_to(q_scale[:, i : i + 1], (TILE, TILE))
        for ref in refs:

            @pl.loop(0, ref.shape[0])
            def _(h):
                for i in range(tiles):
                    rows = slice(i * TILE, (i + 1) * TILE)
                    column = column_buf[rows, :]
                    for t, row in enumerate(k_scale):
                        ref[h, t, rows, :] = ref[h, t, rows, :] * (column * row)


def attention_kernel(tiles, slot_ref, first_ref, second_ref, v_ref, out_hbm, out_buf, sems):
    slots = slot_ref.shape[0] // tiles
    done = first_ref.shape[0]
    heads = done + second_ref.shape[0]
    slot = [[slot_ref[i * slots + n] for n in range(slots)] for i in range(tiles)]
    ones = jnp.ones((TILE, DH), jnp.bfloat16)

    def weights(i, h):
        score_ref, at = (first_ref, h) if h < done else (second_ref, h - done)
        rows = pl.ds(i * TILE, TILE)
        score = [score_ref[at, slot[i][n], rows, :] for n in range(slots)]
        top = jnp.max(functools.reduce(jnp.maximum, score), axis=1, keepdims=True)
        return jnp.concatenate([jnp.exp2(x - top).astype(jnp.bfloat16) for x in score], axis=1)

    def mix(i, h, weight):
        cols = slice(h * DH, (h + 1) * DH)
        value = jnp.concatenate(
            [jnp.concatenate([v_ref[tile_rows(slot[i][n]), cols], ones], axis=1) for n in range(slots)],
            axis=0,
        )
        return jnp.dot(weight, value, preferred_element_type=jnp.float32)

    def finish(i, h, mixed):
        rows = pl.ds(i * TILE, TILE)
        out_buf[rows, h * DH : (h + 1) * DH] = (mixed[:, :DH] / mixed[:, DH:]).astype(jnp.bfloat16)
        if h == heads - 1:
            pltpu.make_async_copy(out_buf.at[rows], out_hbm.at[rows], sems.at[i]).start()

    pairs = [(i, h) for i in range(tiles) for h in range(heads)]
    weight, mixed = {}, {}
    for s in range(len(pairs) + DEPTH + 1):
        if s < len(pairs):
            weight[s] = weights(*pairs[s])
        if DEPTH <= s < len(pairs) + DEPTH:
            mixed[s - DEPTH] = mix(*pairs[s - DEPTH], weight.pop(s - DEPTH))
        if s > DEPTH:
            finish(*pairs[s - DEPTH - 1], mixed.pop(s - DEPTH - 1))
    for i in range(tiles):
        rows = pl.ds(i * TILE, TILE)
        pltpu.make_async_copy(out_buf.at[rows], out_hbm.at[rows], sems.at[i]).wait()


def shards(queries, key_input, value_input, timestep, neighbours, q_gain, k_gain):
    q_rows, k_rows, v_rows = queries[0], key_input[0], value_input[0]
    rows, width = q_rows.shape
    tiles, heads = rows // TILE, width // DH
    slots = neighbours.shape[2]
    groups, devices = lax.axis_size("mp"), lax.axis_size("seq")

    up = [(i, (i + 1) % devices) for i in range(devices)]
    down = [(i, (i - 1) % devices) for i in range(devices)]
    hops = [up] if devices == 2 else [down, up]
    count = len(hops)

    chunk = rows // 2 if tiles % 2 == 0 else TILE
    bf16, f32 = jnp.bfloat16, jnp.float32
    sums, gain, slot, q_all, k_all, *edges = pl.pallas_call(
        functools.partial(sums_kernel, chunk),
        out_shape=[
            pltpu.VMEM((2 * tiles, TILE), f32),
            pltpu.VMEM((2, width), f32),
            pltpu.SMEM((tiles * slots,), jnp.int32),
            pltpu.VMEM((rows, width), bf16),
            pltpu.VMEM((rows, width), bf16),
        ]
        + [pltpu.VMEM((2, TILE, width), bf16)] * count,
        in_specs=[HBM] * 6,
        out_specs=[VMEM, VMEM, SMEM] + [VMEM] * (2 + count),
        scratch_shapes=[
            pltpu.SMEM((slots, 1, tiles), jnp.int32),
            pltpu.VMEM((2, width), f32),
            pltpu.VMEM((2, width), f32),
            pltpu.SemaphoreType.DMA((2, rows // chunk)),
            pltpu.SemaphoreType.DMA((count, 2)),
            pltpu.SemaphoreType.DMA((3,)),
        ],
        compiler_params=pltpu.CompilerParams(vmem_limit_bytes=61 * MIB),
        cost_estimate=pl.CostEstimate(flops=4 * rows * width, bytes_accessed=4 * rows * width, transcendentals=0),
        name="sums",
    )(jnp.transpose(neighbours, (2, 0, 1)), q_gain, k_gain, q_rows, k_rows, v_rows)

    small = pltpu.CompilerParams(vmem_limit_bytes=1 * MIB)
    add = pl.pallas_call(
        add_kernel, out_shape=pltpu.VMEM((2 * tiles, TILE), f32), in_specs=[VMEM] * 2, out_specs=VMEM,
        compiler_params=small, name="add",
    )
    received = lax.ppermute(sums, "mp", [(i, i ^ 1) for i in range(groups)])
    edges = [lax.ppermute(edge, "seq", hop) for edge, hop in zip(edges, hops)]

    key_rows = rows + count * TILE
    early = (heads + 1) // 2
    step = timestep.reshape(1, 1)
    first = pl.pallas_call(
        first_kernel,
        out_shape=pltpu.VMEM((early, key_rows // TILE, rows, TILE), f32),
        in_specs=[VMEM] * 4,
        out_specs=VMEM,
        compiler_params=pltpu.CompilerParams(vmem_limit_bytes=8 * MIB),
        cost_estimate=pl.CostEstimate(flops=2 * rows * rows * early * DH, bytes_accessed=0, transcendentals=0),
        name="first",
    )(step, gain, q_all, k_all)
    received, first = lax.optimization_barrier((received, first))
    half = add(sums, received)
    received = lax.ppermute(half, "mp", [(i, i ^ 2) for i in range(groups)])
    first, second, v_all = pl.pallas_call(
        second_kernel,
        out_shape=[
            pltpu.VMEM((early, key_rows // TILE, rows, TILE), f32),
            pltpu.VMEM((heads - early, key_rows // TILE, rows, TILE), f32),
            pltpu.VMEM((key_rows, width), bf16),
        ],
        in_specs=[VMEM] * 5 + [HBM] + [VMEM] * (count + 1),
        out_specs=[VMEM] * 3,
        input_output_aliases={6 + count: 0},
        scratch_shapes=[pltpu.SemaphoreType.DMA((1 + count,))],
        compiler_params=pltpu.CompilerParams(vmem_limit_bytes=8 * MIB),
        cost_estimate=pl.CostEstimate(flops=2 * rows * rows * early * DH, bytes_accessed=0, transcendentals=0),
        name="second",
    )(half, step, gain, q_all, k_all, v_rows, *edges, first)
    received, first, second, v_all = lax.optimization_barrier((received, first, second, v_all))
    total, border = pl.pallas_call(
        total_kernel,
        out_shape=[pltpu.VMEM((2 * tiles, TILE), f32), pltpu.VMEM((2, TILE), f32)],
        in_specs=[VMEM] * 2, out_specs=[VMEM] * 2, compiler_params=small, name="total",
    )(half, received)
    borders = [lax.ppermute(border, "seq", hop) for hop in hops]

    def scaled(borders, first, second):
        at = 1 + len(borders)
        return pl.pallas_call(
            functools.partial(scale_kernel, width * groups),
            out_shape=[pltpu.VMEM(first.shape, f32), pltpu.VMEM(second.shape, f32)],
            in_specs=[VMEM] * (at + 2),
            out_specs=[VMEM] * 2,
            input_output_aliases={at: 0, at + 1: 1},
            scratch_shapes=[pltpu.VMEM((rows, TILE), f32)],
            compiler_params=small,
            cost_estimate=pl.CostEstimate(flops=rows * rows * heads, bytes_accessed=0, transcendentals=0),
            name="scale",
        )(total, *borders, first, second)

    first, second = scaled([], first, second)
    borders, first, second = lax.optimization_barrier((borders, first, second))
    first, second = scaled(borders, first, second)

    pairs = tiles * slots * TILE * TILE * heads
    mixed = pl.pallas_call(
        functools.partial(attention_kernel, tiles),
        out_shape=jax.ShapeDtypeStruct((rows, width), bf16),
        in_specs=[SMEM] + [VMEM] * 3,
        out_specs=HBM,
        scratch_shapes=[pltpu.VMEM((rows, width), bf16), pltpu.SemaphoreType.DMA((tiles,))],
        compiler_params=pltpu.CompilerParams(vmem_limit_bytes=24 * MIB),
        cost_estimate=pl.CostEstimate(flops=2 * pairs * DH, bytes_accessed=2 * rows * width, transcendentals=pairs),
        name="attention",
    )(slot, first, second, v_all)
    return mixed.reshape(1, rows, width)


def solution(mesh):
    return jax.shard_map(
        shards,
        mesh=mesh,
        in_specs=(
            P("expert", "seq", "mp"),
            P("expert", "seq", "mp"),
            P("expert", "seq", "mp"),
            P("expert"),
            P("expert", "seq", None),
            P(None, "mp"),
            P(None, "mp"),
        ),
        out_specs=P("expert", "seq", "mp"),
        check_vma=False,
    )
```

```python
import functools

import jax
import jax.numpy as jnp
from jax import lax
from jax.experimental import pallas as pl
from jax.experimental.pallas import tpu as pltpu
from jax.sharding import PartitionSpec as P

DH = 128
TILE = 128
EPSILON = 1e-06
SWITCH_STEP = 875
LOG2E = 1.4426950408889634
MIB = 1 << 20
DEPTH = 1

HBM = pl.BlockSpec(memory_space=pltpu.HBM)
VMEM = pl.BlockSpec(memory_space=pltpu.VMEM)
SMEM = pl.BlockSpec(memory_space=pltpu.SMEM)


def tile_rows(index):
    if isinstance(index, int):
        return pl.ds(index * TILE, TILE)
    return pl.ds(pl.multiple_of(index * TILE, TILE), TILE)


def sums_kernel(chunk, near_hbm, gq_hbm, gk_hbm, q_hbm, k_hbm, v_hbm, sums_ref, gain_ref, near_ref,
                q_ref, k_ref, *rest):
    *edges, gq, gk, sems, edge_sems, small_sems = rest
    rows, width = q_hbm.shape
    tiles = rows // TILE
    place = lax.axis_index("seq")
    copies = []
    for a, (src, dst) in enumerate(((q_hbm, q_ref), (k_hbm, k_ref))):
        for j in range(rows // chunk):
            part = pl.ds(j * chunk, chunk)
            copies.append(pltpu.make_async_copy(src.at[part], dst.at[part], sems.at[a, j]))
            copies[-1].start()
    small = [
        pltpu.make_async_copy(src, dst, small_sems.at[a])
        for a, (src, dst) in enumerate(((near_hbm, near_ref), (gq_hbm, gq), (gk_hbm, gk)))
    ]
    for copy in small:
        copy.start()
    edge_copies = []
    for e, edge in enumerate(edges):
        first = jnp.where(place == 0, tiles - 1, 0) if len(edges) == 1 else (0, tiles - 1)[e]
        for a, src in enumerate((k_hbm, v_hbm)):
            edge_copies.append(pltpu.make_async_copy(src.at[tile_rows(first)], edge.at[a], edge_sems.at[e, a]))
            edge_copies[-1].start()
    diagonal = lax.broadcasted_iota(jnp.int32, (TILE, TILE), 0) == lax.broadcasted_iota(
        jnp.int32, (TILE, TILE), 1
    )
    for a, buf in enumerate((q_ref, k_ref)):
        for t in range(tiles):
            if t * TILE % chunk == 0:
                copies[a * (rows // chunk) + t * TILE // chunk].wait()
            total = 0.0
            for j in range(width // DH):
                x = buf[t * TILE : (t + 1) * TILE, j * DH : (j + 1) * DH].astype(jnp.float32)
                total = total + x * x
            total = jnp.sum(total, axis=1, keepdims=True)
            total = jnp.sum(jnp.where(diagonal, total, 0.0), axis=0, keepdims=True)
            sums_ref[a * tiles + t : a * tiles + t + 1, :] = total
        if a == 0:
            for copy in small:
                copy.wait()
            gain_ref[...] = gq[...] * gk[...] * (DH ** -0.5 * LOG2E)
    for copy in edge_copies:
        copy.wait()


def add_kernel(a_ref, b_ref, out_ref):
    out_ref[...] = a_ref[...] + b_ref[...]


def total_kernel(a_ref, b_ref, out_ref, border_ref):
    total = a_ref[...] + b_ref[...]
    out_ref[...] = total
    tiles = total.shape[0] // 2
    border_ref[0:1, :] = total[tiles : tiles + 1]
    border_ref[1:2, :] = total[2 * tiles - 1 : 2 * tiles]


def expert_gain(step_ref, gain_ref):
    return jnp.where(step_ref[...] >= SWITCH_STEP, gain_ref[0:1, :], gain_ref[1:2, :])


def own_scores(gain, q_ref, k_ref, score_ref, at, h):
    cols = slice(h * DH, (h + 1) * DH)
    query = (q_ref[:, cols].astype(jnp.float32) * gain[:, cols]).astype(jnp.bfloat16)
    rows = k_ref.shape[0]
    for j in range(0, rows, 2 * TILE):
        end = min(j + 2 * TILE, rows)
        score = lax.dot_general(
            query, k_ref[j:end, cols], (((1,), (1,)), ((), ())), preferred_element_type=jnp.float32
        )
        for c in range(0, end - j, TILE):
            score_ref[at, (j + c) // TILE] = score[:, c : c + TILE]


def first_kernel(step_ref, gain_ref, q_ref, k_ref, score_ref):
    gain = expert_gain(step_ref, gain_ref)
    for h in range(score_ref.shape[0]):
        own_scores(gain, q_ref, k_ref, score_ref, h, h)


def second_kernel(half_ref, step_ref, gain_ref, q_ref, k_ref, v_hbm, *rest):
    del half_ref
    *edges, given_ref, first_ref, score_ref, v_ref, sems = rest
    del given_ref
    rows = q_ref.shape[0]
    copies = [pltpu.make_async_copy(v_hbm, v_ref.at[pl.ds(0, rows)], sems.at[0])]
    for e, edge in enumerate(edges):
        part = pl.ds(rows + e * TILE, TILE)
        copies.append(pltpu.make_async_copy(edge.at[1], v_ref.at[part], sems.at[1 + e]))
    for copy in copies:
        copy.start()
    gain = expert_gain(step_ref, gain_ref)
    done = first_ref.shape[0]
    for h in range(done + score_ref.shape[0]):
        cols = slice(h * DH, (h + 1) * DH)
        out_ref, at = (first_ref, h) if h < done else (score_ref, h - done)
        if h >= done:
            own_scores(gain, q_ref, k_ref, score_ref, at, h)
        query = (q_ref[:, cols].astype(jnp.float32) * gain[:, cols]).astype(jnp.bfloat16)
        for e, edge in enumerate(edges):
            out_ref[at, rows // TILE + e] = lax.dot_general(
                query, edge[0, :, cols], (((1,), (1,)), ((), ())), preferred_element_type=jnp.float32
            )
    for copy in copies:
        copy.wait()


def scale_kernel(full_width, sums_ref, *rest):
    *borders, _, _, first_ref, second_ref, column_buf = rest
    tiles = sums_ref.shape[0] // 2

    def scale(sums):
        return lax.rsqrt(sums * (1.0 / full_width) + EPSILON)

    refs = (first_ref, second_ref)
    if borders:
        if len(borders) == 1:
            place = lax.axis_index("seq")
            k_scale = [scale(jnp.where(place == 0, borders[0][0:1, :], borders[0][1:2, :]))]
        else:
            k_scale = [scale(borders[0][0:1, :]), scale(borders[1][1:2, :])]
        for t, row in enumerate(k_scale):
            for ref in refs:
                for h in range(ref.shape[0]):
                    ref[h, tiles + t] = ref[h, tiles + t] * row
    else:
        k_scale = [scale(sums_ref[tiles + t : tiles + t + 1, :]) for t in range(tiles)]
        q_scale = scale(sums_ref[0:tiles, :])
        q_scale = jnp.concatenate([q_scale, jnp.zeros((8 - tiles % 8, TILE), jnp.float32)], axis=0).T
        k_scale += [jnp.ones((1, TILE), jnp.float32)] * (first_ref.shape[1] - tiles)
        for i in range(tiles):
            column_buf[i * TILE : (i + 1) * TILE, :] = jnp.broadcast_to(q_scale[:, i : i + 1], (TILE, TILE))
        for ref in refs:

            @pl.loop(0, ref.shape[0])
            def _(h):
                for i in range(tiles):
                    rows = slice(i * TILE, (i + 1) * TILE)
                    column = column_buf[rows, :]
                    for t, row in enumerate(k_scale):
                        ref[h, t, rows, :] = ref[h, t, rows, :] * (column * row)


def attention_kernel(count, near_ref, first_ref, second_ref, v_ref, out_hbm, out_buf, sems):
    slots, _, tiles = near_ref.shape
    place = lax.axis_index("seq")
    done = first_ref.shape[0]
    heads = done + second_ref.shape[0]

    def where_at(i, n):
        local = near_ref[n, 0, i] - place * tiles
        return jnp.where(local < 0, tiles + count - 1, jnp.minimum(local, tiles))

    slot = [[where_at(i, n) for n in range(slots)] for i in range(tiles)]
    ones = jnp.ones((TILE, DH), jnp.bfloat16)

    def weights(i, h):
        score_ref, at = (first_ref, h) if h < done else (second_ref, h - done)
        rows = pl.ds(i * TILE, TILE)
        score = [score_ref[at, slot[i][n], rows, :] for n in range(slots)]
        top = jnp.max(functools.reduce(jnp.maximum, score), axis=1, keepdims=True)
        return jnp.concatenate([jnp.exp2(x - top).astype(jnp.bfloat16) for x in score], axis=1)

    def mix(i, h, weight):
        cols = slice(h * DH, (h + 1) * DH)
        value = jnp.concatenate(
            [jnp.concatenate([v_ref[tile_rows(slot[i][n]), cols], ones], axis=1) for n in range(slots)],
            axis=0,
        )
        return jnp.dot(weight, value, preferred_element_type=jnp.float32)

    def finish(i, h, mixed):
        rows = pl.ds(i * TILE, TILE)
        out_buf[rows, h * DH : (h + 1) * DH] = (mixed[:, :DH] / mixed[:, DH:]).astype(jnp.bfloat16)
        if h == heads - 1:
            pltpu.make_async_copy(out_buf.at[rows], out_hbm.at[rows], sems.at[i]).start()

    pairs = [(i, h) for i in range(tiles) for h in range(heads)]
    weight, mixed = {}, {}
    for s in range(len(pairs) + DEPTH + 1):
        if s < len(pairs):
            weight[s] = weights(*pairs[s])
        if DEPTH <= s < len(pairs) + DEPTH:
            mixed[s - DEPTH] = mix(*pairs[s - DEPTH], weight.pop(s - DEPTH))
        if s > DEPTH:
            finish(*pairs[s - DEPTH - 1], mixed.pop(s - DEPTH - 1))
    for i in range(tiles):
        rows = pl.ds(i * TILE, TILE)
        pltpu.make_async_copy(out_buf.at[rows], out_hbm.at[rows], sems.at[i]).wait()


def shards(queries, key_input, value_input, timestep, neighbours, q_gain, k_gain):
    q_rows, k_rows, v_rows = queries[0], key_input[0], value_input[0]
    rows, width = q_rows.shape
    tiles, heads = rows // TILE, width // DH
    slots = neighbours.shape[2]
    groups, devices = lax.axis_size("mp"), lax.axis_size("seq")

    up = [(i, (i + 1) % devices) for i in range(devices)]
    down = [(i, (i - 1) % devices) for i in range(devices)]
    hops = [up] if devices == 2 else [down, up]
    count = len(hops)

    chunk = rows // 2 if tiles % 2 == 0 else TILE
    bf16, f32 = jnp.bfloat16, jnp.float32
    sums, gain, slot, q_all, k_all, *edges = pl.pallas_call(
        functools.partial(sums_kernel, chunk),
        out_shape=[
            pltpu.VMEM((2 * tiles, TILE), f32),
            pltpu.VMEM((2, width), f32),
            pltpu.SMEM((slots, 1, tiles), jnp.int32),
            pltpu.VMEM((rows, width), bf16),
            pltpu.VMEM((rows, width), bf16),
        ]
        + [pltpu.VMEM((2, TILE, width), bf16)] * count,
        in_specs=[HBM] * 6,
        out_specs=[VMEM, VMEM, SMEM] + [VMEM] * (2 + count),
        scratch_shapes=[
            pltpu.VMEM((2, width), f32),
            pltpu.VMEM((2, width), f32),
            pltpu.SemaphoreType.DMA((2, rows // chunk)),
            pltpu.SemaphoreType.DMA((count, 2)),
            pltpu.SemaphoreType.DMA((3,)),
        ],
        compiler_params=pltpu.CompilerParams(vmem_limit_bytes=61 * MIB),
        cost_estimate=pl.CostEstimate(flops=4 * rows * width, bytes_accessed=4 * rows * width, transcendentals=0),
        name="sums",
    )(jnp.transpose(neighbours, (2, 0, 1)), q_gain, k_gain, q_rows, k_rows, v_rows)

    small = pltpu.CompilerParams(vmem_limit_bytes=1 * MIB)
    add = pl.pallas_call(
        add_kernel, out_shape=pltpu.VMEM((2 * tiles, TILE), f32), in_specs=[VMEM] * 2, out_specs=VMEM,
        compiler_params=small, name="add",
    )
    received = lax.ppermute(sums, "mp", [(i, i ^ 1) for i in range(groups)])
    edges = [lax.ppermute(edge, "seq", hop) for edge, hop in zip(edges, hops)]

    key_rows = rows + count * TILE
    early = (heads + 1) // 2
    step = timestep.reshape(1, 1)
    first = pl.pallas_call(
        first_kernel,
        out_shape=pltpu.VMEM((early, key_rows // TILE, rows, TILE), f32),
        in_specs=[VMEM] * 4,
        out_specs=VMEM,
        compiler_params=pltpu.CompilerParams(vmem_limit_bytes=8 * MIB),
        cost_estimate=pl.CostEstimate(flops=2 * rows * rows * early * DH, bytes_accessed=0, transcendentals=0),
        name="first",
    )(step, gain, q_all, k_all)
    received, first = lax.optimization_barrier((received, first))
    half = add(sums, received)
    received = lax.ppermute(half, "mp", [(i, i ^ 2) for i in range(groups)])
    first, second, v_all = pl.pallas_call(
        second_kernel,
        out_shape=[
            pltpu.VMEM((early, key_rows // TILE, rows, TILE), f32),
            pltpu.VMEM((heads - early, key_rows // TILE, rows, TILE), f32),
            pltpu.VMEM((key_rows, width), bf16),
        ],
        in_specs=[VMEM] * 5 + [HBM] + [VMEM] * (count + 1),
        out_specs=[VMEM] * 3,
        input_output_aliases={6 + count: 0},
        scratch_shapes=[pltpu.SemaphoreType.DMA((1 + count,))],
        compiler_params=pltpu.CompilerParams(vmem_limit_bytes=8 * MIB),
        cost_estimate=pl.CostEstimate(flops=2 * rows * rows * early * DH, bytes_accessed=0, transcendentals=0),
        name="second",
    )(half, step, gain, q_all, k_all, v_rows, *edges, first)
    received, first, second, v_all = lax.optimization_barrier((received, first, second, v_all))
    total, border = pl.pallas_call(
        total_kernel,
        out_shape=[pltpu.VMEM((2 * tiles, TILE), f32), pltpu.VMEM((2, TILE), f32)],
        in_specs=[VMEM] * 2, out_specs=[VMEM] * 2, compiler_params=small, name="total",
    )(half, received)
    borders = [lax.ppermute(border, "seq", hop) for hop in hops]

    def scaled(borders, first, second):
        at = 1 + len(borders)
        return pl.pallas_call(
            functools.partial(scale_kernel, width * groups),
            out_shape=[pltpu.VMEM(first.shape, f32), pltpu.VMEM(second.shape, f32)],
            in_specs=[VMEM] * (at + 2),
            out_specs=[VMEM] * 2,
            input_output_aliases={at: 0, at + 1: 1},
            scratch_shapes=[pltpu.VMEM((rows, TILE), f32)],
            compiler_params=small,
            cost_estimate=pl.CostEstimate(flops=rows * rows * heads, bytes_accessed=0, transcendentals=0),
            name="scale",
        )(total, *borders, first, second)

    first, second = scaled([], first, second)
    borders, first, second = lax.optimization_barrier((borders, first, second))
    first, second = scaled(borders, first, second)

    pairs = tiles * slots * TILE * TILE * heads
    mixed = pl.pallas_call(
        functools.partial(attention_kernel, count),
        out_shape=jax.ShapeDtypeStruct((rows, width), bf16),
        in_specs=[SMEM] + [VMEM] * 3,
        out_specs=HBM,
        scratch_shapes=[pltpu.VMEM((rows, width), bf16), pltpu.SemaphoreType.DMA((tiles,))],
        compiler_params=pltpu.CompilerParams(vmem_limit_bytes=24 * MIB),
        cost_estimate=pl.CostEstimate(flops=2 * pairs * DH, bytes_accessed=2 * rows * width, transcendentals=pairs),
        name="attention",
    )(slot, first, second, v_all)
    return mixed.reshape(1, rows, width)


def solution(mesh):
    return jax.shard_map(
        shards,
        mesh=mesh,
        in_specs=(
            P("expert", "seq", "mp"),
            P("expert", "seq", "mp"),
            P("expert", "seq", "mp"),
            P("expert"),
            P("expert", "seq", None),
            P(None, "mp"),
            P(None, "mp"),
        ),
        out_specs=P("expert", "seq", "mp"),
        check_vma=False,
    )
```

```python
import functools

import jax
import jax.numpy as jnp
from jax import lax
from jax.experimental import pallas as pl
from jax.experimental.pallas import tpu as pltpu
from jax.sharding import PartitionSpec as P

DH = 128
TILE = 128
EPSILON = 1e-06
SWITCH_STEP = 875
LOG2E = 1.4426950408889634
MIB = 1 << 20
DEPTH = 1

HBM = pl.BlockSpec(memory_space=pltpu.HBM)
VMEM = pl.BlockSpec(memory_space=pltpu.VMEM)
SMEM = pl.BlockSpec(memory_space=pltpu.SMEM)


def tile_rows(index):
    if isinstance(index, int):
        return pl.ds(index * TILE, TILE)
    return pl.ds(pl.multiple_of(index * TILE, TILE), TILE)


def sums_kernel(chunk, near_hbm, gq_hbm, gk_hbm, q_hbm, k_hbm, v_hbm, sums_ref, gain_ref, slot_ref,
                q_ref, k_ref, *rest):
    *edges, near, gq, gk, sems, edge_sems, small_sems = rest
    rows, width = q_hbm.shape
    tiles, slots = rows // TILE, near_hbm.shape[0]
    place = lax.axis_index("seq")
    copies = []
    for a, (src, dst) in enumerate(((q_hbm, q_ref), (k_hbm, k_ref))):
        for j in range(rows // chunk):
            part = pl.ds(j * chunk, chunk)
            copies.append(pltpu.make_async_copy(src.at[part], dst.at[part], sems.at[a, j]))
            copies[-1].start()
    small = [
        pltpu.make_async_copy(src, dst, small_sems.at[a])
        for a, (src, dst) in enumerate(((near_hbm, near), (gq_hbm, gq), (gk_hbm, gk)))
    ]
    for copy in small:
        copy.start()
    edge_copies = []
    for e, edge in enumerate(edges):
        first = jnp.where(place == 0, tiles - 1, 0) if len(edges) == 1 else (0, tiles - 1)[e]
        for a, src in enumerate((k_hbm, v_hbm)):
            edge_copies.append(pltpu.make_async_copy(src.at[tile_rows(first)], edge.at[a], edge_sems.at[e, a]))
            edge_copies[-1].start()
    diagonal = lax.broadcasted_iota(jnp.int32, (TILE, TILE), 0) == lax.broadcasted_iota(
        jnp.int32, (TILE, TILE), 1
    )
    for a, buf in enumerate((q_ref, k_ref)):
        for j in range(rows // chunk):
            copies[a * (rows // chunk) + j].wait()
            per = chunk // TILE

            @pl.loop(0, per // 3)
            def _(b):
                for c in range(3):
                    t = j * per + b * 3 + c
                    total = 0.0
                    for p in range(width // DH):
                        x = buf[tile_rows(t), p * DH : (p + 1) * DH].astype(jnp.float32)
                        total = total + x * x
                    total = jnp.sum(total, axis=1, keepdims=True)
                    total = jnp.sum(jnp.where(diagonal, total, 0.0), axis=0, keepdims=True)
                    sums_ref[pl.ds(a * tiles + t, 1), :] = total

        if a == 0:
            for copy in small:
                copy.wait()
            gain_ref[...] = gq[...] * gk[...] * (DH ** -0.5 * LOG2E)
            for i in range(tiles):
                for n in range(slots):
                    local = near[n, 0, i] - place * tiles
                    local = jnp.where(local < 0, tiles + len(edges) - 1, jnp.minimum(local, tiles))
                    slot_ref[i * slots + n] = local
    for copy in edge_copies:
        copy.wait()


def add_kernel(a_ref, b_ref, out_ref):
    out_ref[...] = a_ref[...] + b_ref[...]


def total_kernel(a_ref, b_ref, out_ref, border_ref):
    total = a_ref[...] + b_ref[...]
    out_ref[...] = total
    tiles = total.shape[0] // 2
    border_ref[0:1, :] = total[tiles : tiles + 1]
    border_ref[1:2, :] = total[2 * tiles - 1 : 2 * tiles]


def expert_gain(step_ref, gain_ref):
    return jnp.where(step_ref[...] >= SWITCH_STEP, gain_ref[0:1, :], gain_ref[1:2, :])


def own_scores(gain, q_ref, k_ref, score_ref, at, h):
    cols = slice(h * DH, (h + 1) * DH)
    query = (q_ref[:, cols].astype(jnp.float32) * gain[:, cols]).astype(jnp.bfloat16)
    rows = k_ref.shape[0]
    for j in range(0, rows, 2 * TILE):
        end = min(j + 2 * TILE, rows)
        score = lax.dot_general(
            query, k_ref[j:end, cols], (((1,), (1,)), ((), ())), preferred_element_type=jnp.float32
        )
        for c in range(0, end - j, TILE):
            score_ref[at, (j + c) // TILE] = score[:, c : c + TILE]


def first_kernel(step_ref, gain_ref, q_ref, k_ref, score_ref):
    gain = expert_gain(step_ref, gain_ref)
    for h in range(score_ref.shape[0]):
        own_scores(gain, q_ref, k_ref, score_ref, h, h)


def second_kernel(half_ref, step_ref, gain_ref, q_ref, k_ref, v_hbm, *rest):
    del half_ref
    *edges, given_ref, first_ref, score_ref, v_ref, sems = rest
    del given_ref
    rows = q_ref.shape[0]
    copies = [pltpu.make_async_copy(v_hbm, v_ref.at[pl.ds(0, rows)], sems.at[0])]
    for e, edge in enumerate(edges):
        part = pl.ds(rows + e * TILE, TILE)
        copies.append(pltpu.make_async_copy(edge.at[1], v_ref.at[part], sems.at[1 + e]))
    for copy in copies:
        copy.start()
    gain = expert_gain(step_ref, gain_ref)
    done = first_ref.shape[0]
    for h in range(done + score_ref.shape[0]):
        cols = slice(h * DH, (h + 1) * DH)
        out_ref, at = (first_ref, h) if h < done else (score_ref, h - done)
        if h >= done:
            own_scores(gain, q_ref, k_ref, score_ref, at, h)
        query = (q_ref[:, cols].astype(jnp.float32) * gain[:, cols]).astype(jnp.bfloat16)
        for e, edge in enumerate(edges):
            out_ref[at, rows // TILE + e] = lax.dot_general(
                query, edge[0, :, cols], (((1,), (1,)), ((), ())), preferred_element_type=jnp.float32
            )
    for copy in copies:
        copy.wait()


def scale_kernel(full_width, sums_ref, *rest):
    *borders, _, _, first_ref, second_ref, column_buf = rest
    tiles = sums_ref.shape[0] // 2

    def scale(sums):
        return lax.rsqrt(sums * (1.0 / full_width) + EPSILON)

    refs = (first_ref, second_ref)
    if borders:
        if len(borders) == 1:
            place = lax.axis_index("seq")
            k_scale = [scale(jnp.where(place == 0, borders[0][0:1, :], borders[0][1:2, :]))]
        else:
            k_scale = [scale(borders[0][0:1, :]), scale(borders[1][1:2, :])]
        for t, row in enumerate(k_scale):
            for ref in refs:
                for h in range(ref.shape[0]):
                    ref[h, tiles + t] = ref[h, tiles + t] * row
    else:
        k_scale = [scale(sums_ref[tiles + t : tiles + t + 1, :]) for t in range(tiles)]
        q_scale = scale(sums_ref[0:tiles, :])
        q_scale = jnp.concatenate([q_scale, jnp.zeros((8 - tiles % 8, TILE), jnp.float32)], axis=0).T
        k_scale += [jnp.ones((1, TILE), jnp.float32)] * (first_ref.shape[1] - tiles)
        for i in range(tiles):
            column_buf[i * TILE : (i + 1) * TILE, :] = jnp.broadcast_to(q_scale[:, i : i + 1], (TILE, TILE))
        for ref in refs:

            @pl.loop(0, ref.shape[0])
            def _(h):
                for i in range(tiles):
                    rows = slice(i * TILE, (i + 1) * TILE)
                    column = column_buf[rows, :]
                    for t, row in enumerate(k_scale):
                        ref[h, t, rows, :] = ref[h, t, rows, :] * (column * row)


def attention_kernel(tiles, slot_ref, first_ref, second_ref, v_ref, out_hbm, out_buf, sems):
    slots = slot_ref.shape[0] // tiles
    done = first_ref.shape[0]
    heads = done + second_ref.shape[0]
    slot = [[slot_ref[i * slots + n] for n in range(slots)] for i in range(tiles)]
    ones = jnp.ones((TILE, DH), jnp.bfloat16)

    def weights(i, h):
        score_ref, at = (first_ref, h) if h < done else (second_ref, h - done)
        rows = pl.ds(i * TILE, TILE)
        score = [score_ref[at, slot[i][n], rows, :] for n in range(slots)]
        top = jnp.max(functools.reduce(jnp.maximum, score), axis=1, keepdims=True)
        return jnp.concatenate([jnp.exp2(x - top).astype(jnp.bfloat16) for x in score], axis=1)

    def mix(i, h, weight):
        cols = slice(h * DH, (h + 1) * DH)
        value = jnp.concatenate(
            [jnp.concatenate([v_ref[tile_rows(slot[i][n]), cols], ones], axis=1) for n in range(slots)],
            axis=0,
        )
        return jnp.dot(weight, value, preferred_element_type=jnp.float32)

    def finish(i, h, mixed):
        rows = pl.ds(i * TILE, TILE)
        out_buf[rows, h * DH : (h + 1) * DH] = (mixed[:, :DH] / mixed[:, DH:]).astype(jnp.bfloat16)
        if h == heads - 1:
            pltpu.make_async_copy(out_buf.at[rows], out_hbm.at[rows], sems.at[i]).start()

    pairs = [(i, h) for i in range(tiles) for h in range(heads)]
    weight, mixed = {}, {}
    for s in range(len(pairs) + DEPTH + 1):
        if s < len(pairs):
            weight[s] = weights(*pairs[s])
        if DEPTH <= s < len(pairs) + DEPTH:
            mixed[s - DEPTH] = mix(*pairs[s - DEPTH], weight.pop(s - DEPTH))
        if s > DEPTH:
            finish(*pairs[s - DEPTH - 1], mixed.pop(s - DEPTH - 1))
    for i in range(tiles):
        rows = pl.ds(i * TILE, TILE)
        pltpu.make_async_copy(out_buf.at[rows], out_hbm.at[rows], sems.at[i]).wait()


def shards(queries, key_input, value_input, timestep, neighbours, q_gain, k_gain):
    q_rows, k_rows, v_rows = queries[0], key_input[0], value_input[0]
    rows, width = q_rows.shape
    tiles, heads = rows // TILE, width // DH
    slots = neighbours.shape[2]
    groups, devices = lax.axis_size("mp"), lax.axis_size("seq")

    up = [(i, (i + 1) % devices) for i in range(devices)]
    down = [(i, (i - 1) % devices) for i in range(devices)]
    hops = [up] if devices == 2 else [down, up]
    count = len(hops)

    chunk = rows // 2 if tiles % 2 == 0 else TILE
    bf16, f32 = jnp.bfloat16, jnp.float32
    sums, gain, slot, q_all, k_all, *edges = pl.pallas_call(
        functools.partial(sums_kernel, chunk),
        out_shape=[
            pltpu.VMEM((2 * tiles, TILE), f32),
            pltpu.VMEM((2, width), f32),
            pltpu.SMEM((tiles * slots,), jnp.int32),
            pltpu.VMEM((rows, width), bf16),
            pltpu.VMEM((rows, width), bf16),
        ]
        + [pltpu.VMEM((2, TILE, width), bf16)] * count,
        in_specs=[HBM] * 6,
        out_specs=[VMEM, VMEM, SMEM] + [VMEM] * (2 + count),
        scratch_shapes=[
            pltpu.SMEM((slots, 1, tiles), jnp.int32),
            pltpu.VMEM((2, width), f32),
            pltpu.VMEM((2, width), f32),
            pltpu.SemaphoreType.DMA((2, rows // chunk)),
            pltpu.SemaphoreType.DMA((count, 2)),
            pltpu.SemaphoreType.DMA((3,)),
        ],
        compiler_params=pltpu.CompilerParams(vmem_limit_bytes=61 * MIB),
        cost_estimate=pl.CostEstimate(flops=4 * rows * width, bytes_accessed=4 * rows * width, transcendentals=0),
        name="sums",
    )(jnp.transpose(neighbours, (2, 0, 1)), q_gain, k_gain, q_rows, k_rows, v_rows)

    small = pltpu.CompilerParams(vmem_limit_bytes=1 * MIB)
    add = pl.pallas_call(
        add_kernel, out_shape=pltpu.VMEM((2 * tiles, TILE), f32), in_specs=[VMEM] * 2, out_specs=VMEM,
        compiler_params=small, name="add",
    )
    received = lax.ppermute(sums, "mp", [(i, i ^ 1) for i in range(groups)])
    edges = [lax.ppermute(edge, "seq", hop) for edge, hop in zip(edges, hops)]

    key_rows = rows + count * TILE
    early = (heads + 1) // 2
    step = timestep.reshape(1, 1)
    first = pl.pallas_call(
        first_kernel,
        out_shape=pltpu.VMEM((early, key_rows // TILE, rows, TILE), f32),
        in_specs=[VMEM] * 4,
        out_specs=VMEM,
        compiler_params=pltpu.CompilerParams(vmem_limit_bytes=8 * MIB),
        cost_estimate=pl.CostEstimate(flops=2 * rows * rows * early * DH, bytes_accessed=0, transcendentals=0),
        name="first",
    )(step, gain, q_all, k_all)
    received, first = lax.optimization_barrier((received, first))
    half = add(sums, received)
    received = lax.ppermute(half, "mp", [(i, i ^ 2) for i in range(groups)])
    first, second, v_all = pl.pallas_call(
        second_kernel,
        out_shape=[
            pltpu.VMEM((early, key_rows // TILE, rows, TILE), f32),
            pltpu.VMEM((heads - early, key_rows // TILE, rows, TILE), f32),
            pltpu.VMEM((key_rows, width), bf16),
        ],
        in_specs=[VMEM] * 5 + [HBM] + [VMEM] * (count + 1),
        out_specs=[VMEM] * 3,
        input_output_aliases={6 + count: 0},
        scratch_shapes=[pltpu.SemaphoreType.DMA((1 + count,))],
        compiler_params=pltpu.CompilerParams(vmem_limit_bytes=8 * MIB),
        cost_estimate=pl.CostEstimate(flops=2 * rows * rows * early * DH, bytes_accessed=0, transcendentals=0),
        name="second",
    )(half, step, gain, q_all, k_all, v_rows, *edges, first)
    received, first, second, v_all = lax.optimization_barrier((received, first, second, v_all))
    total, border = pl.pallas_call(
        total_kernel,
        out_shape=[pltpu.VMEM((2 * tiles, TILE), f32), pltpu.VMEM((2, TILE), f32)],
        in_specs=[VMEM] * 2, out_specs=[VMEM] * 2, compiler_params=small, name="total",
    )(half, received)
    borders = [lax.ppermute(border, "seq", hop) for hop in hops]

    def scaled(borders, first, second):
        at = 1 + len(borders)
        return pl.pallas_call(
            functools.partial(scale_kernel, width * groups),
            out_shape=[pltpu.VMEM(first.shape, f32), pltpu.VMEM(second.shape, f32)],
            in_specs=[VMEM] * (at + 2),
            out_specs=[VMEM] * 2,
            input_output_aliases={at: 0, at + 1: 1},
            scratch_shapes=[pltpu.VMEM((rows, TILE), f32)],
            compiler_params=small,
            cost_estimate=pl.CostEstimate(flops=rows * rows * heads, bytes_accessed=0, transcendentals=0),
            name="scale",
        )(total, *borders, first, second)

    first, second = scaled([], first, second)
    borders, first, second = lax.optimization_barrier((borders, first, second))
    first, second = scaled(borders, first, second)

    pairs = tiles * slots * TILE * TILE * heads
    mixed = pl.pallas_call(
        functools.partial(attention_kernel, tiles),
        out_shape=jax.ShapeDtypeStruct((rows, width), bf16),
        in_specs=[SMEM] + [VMEM] * 3,
        out_specs=HBM,
        scratch_shapes=[pltpu.VMEM((rows, width), bf16), pltpu.SemaphoreType.DMA((tiles,))],
        compiler_params=pltpu.CompilerParams(vmem_limit_bytes=24 * MIB),
        cost_estimate=pl.CostEstimate(flops=2 * pairs * DH, bytes_accessed=2 * rows * width, transcendentals=pairs),
        name="attention",
    )(slot, first, second, v_all)
    return mixed.reshape(1, rows, width)


def solution(mesh):
    return jax.shard_map(
        shards,
        mesh=mesh,
        in_specs=(
            P("expert", "seq", "mp"),
            P("expert", "seq", "mp"),
            P("expert", "seq", "mp"),
            P("expert"),
            P("expert", "seq", None),
            P(None, "mp"),
            P(None, "mp"),
        ),
        out_specs=P("expert", "seq", "mp"),
        check_vma=False,
    )
```
